512 devices in a mesh: grid: 64 (over y, z), batch: 8 (over x, core).
Axes of the slice: x: 4, y: 4, z: 16, core: 2. Of those that a mesh axis runs over, the one named last changes fastest.
Arguments:
- inputs: bfloat16 [8, 256, 65536], P('batch', None, 'grid'), may hold values from -6 to 6
- cotangent: bfloat16 [8, 256, 65536], P('batch', None, 'grid'), may hold values from -8 to 8
- weights: bfloat16 [512, 8, 9216], P('grid', 'batch'), may hold values from -0.375 to 0.375
- gate_logits: float32 [8, 256, 2], replicated, may hold values from -5 to 5
- routes: int32 [8, 256, 2], replicated, may hold values from 0 to 511, as said below
Outputs:
- d_inputs: bfloat16 [8, 256, 65536], P('batch', None, 'grid')
- d_weights: float32 [512, 8, 9216], P('grid', 'batch')
- gate_grad: float32 [8, 256, 2], P(None, 'grid')
The draws below stay inside these ranges and needn't reach their ends.
Inputs may be any that keep to these rules, and one draw needn't show every extreme that they name: Expert e is owned by grid index e // 8. The 64 routes of the patches g * 4 to (g + 1) * 4 - 1 of all samples name experts of one owner at most 1 times, for every grid index g; in every draw some owner is named exactly 1 times by the routes of every grid index. The 2 routes of a patch name different experts.
All inputs are finite; a program needn't handle non-finite values.
Results may differ from the reference program's by a relative error of at most 0.0051.
Values may be sent and summed in bfloat16 or wider, within the bound.
A program may use at most 128 MiB of HBM per device.

```python
import jax
import jax.numpy as jnp
from jax import lax

C = 256
CG = 32
SIDE = 16
TOPK = 2
EXP_DEV = 8
PCOL = 4
PIX = 256
GROUPS = 8
EXPERTS = 512
BATCH = 8
NPATCH = 256
ROUTES = 64
N_GRID = 64
N_BATCH = 8


def draw_cotangent(key, part):
    channel_pos = jnp.arange(C, dtype=jnp.float32) / (C - 1)
    full_shape = (BATCH, C, NPATCH * PIX)
    channel_scale = 0.6 * 3.0 ** channel_pos
    values_drawn = jax.random.truncated_normal(key, -4.0, 4.0, full_shape, jnp.float32)
    return (values_drawn * channel_scale[None, :, None]).astype(jnp.bfloat16)


def draw_routes(key, part):
    hot_owner = jax.random.randint(jax.random.fold_in(key, 11), (), 0, N_GRID)
    tile_keys = jax.random.split(jax.random.fold_in(key, 12), N_GRID)
    owners = jax.vmap(lambda tile_key: jax.random.permutation(tile_key, N_GRID))(tile_keys)
    leading = owners[:, :1]
    owners = jnp.where(owners == hot_owner, leading, owners)
    position = jnp.arange(N_GRID)[None, :]
    owners = jnp.where(position == 0, hot_owner, owners)
    order_keys = jax.random.split(jax.random.fold_in(key, 13), N_GRID)
    route_order = jax.vmap(lambda tile_key: jax.random.permutation(tile_key, ROUTES))(order_keys)
    owner_of = jnp.take_along_axis(owners, route_order % N_GRID, axis=1)
    local_base = jax.random.randint(jax.random.fold_in(key, 14), (N_GRID, BATCH * PCOL, 1), 0, EXP_DEV)
    stride = 2 * jax.random.randint(jax.random.fold_in(key, 15), (N_GRID, BATCH * PCOL, 1), 0, max(EXP_DEV // 2, 1)) + 1
    local_index = (local_base + stride * jnp.arange(TOPK)[None, None, :]) % EXP_DEV
    experts = owner_of.reshape(N_GRID, BATCH * PCOL, TOPK) * EXP_DEV + local_index
    experts = experts.reshape(N_GRID, BATCH, PCOL, TOPK).transpose(1, 0, 2, 3)
    return experts.reshape(BATCH, NPATCH, TOPK).astype(jnp.int32)


def levels(stream_key, extent, cuts, least, top_value):
    loudness = 1.0
    for dim, blocks in cuts:
        draws = jax.random.uniform(jax.random.fold_in(jax.random.fold_in(stream_key, 6), dim), (blocks,), jnp.float32, least / len(cuts), top_value / len(cuts))
        loudness = loudness * jnp.repeat(jnp.exp(draws), extent[dim] // blocks).reshape((-1,) + (1,) * (len(extent) - 1 - dim))
    return loudness


def bell_draw(stream_key, shape, scale, reach, cuts=(), held_as=jnp.bfloat16):
    loudness = levels(stream_key, shape, cuts, -0.22, 0.18) if cuts else 1.0
    entries = jax.random.normal(stream_key, shape, jnp.float32) * scale * loudness
    return jnp.minimum(jnp.maximum(entries, -reach), reach).astype(held_as)


def setup_inputs(seed: int = 0) -> dict:
    key_of = jax.random.split(jax.random.key(seed), 6)
    inputs = bell_draw(key_of[0], (BATCH, C, NPATCH * PIX), 1.0, 6.0, ((0, 8), (2, 64)))
    cotangent = draw_cotangent(jax.random.fold_in(key_of[5], 71), 0)
    weights = bell_draw(key_of[2], (EXPERTS, GROUPS, CG * CG * 9), (9 * CG) ** -0.5, 0.375, ((0, 64), (1, 8)))
    gate_logits = bell_draw(key_of[3], (BATCH, NPATCH, TOPK), 1.5, 5.0, (), jnp.float32)
    routes = draw_routes(jax.random.fold_in(key_of[5], 71), 0)
    return {"inputs": inputs, "cotangent": cotangent, "weights": weights, "gate_logits": gate_logits, "routes": routes}


def shifted(values, row_shift, column_shift):
    margin = SIDE + 1
    padded = jnp.pad(values, [(0, 0)] * (values.ndim - 1) + [(margin, margin)])
    first_index = margin + row_shift * SIDE + column_shift
    moved = lax.slice_in_dim(padded, first_index, first_index + PIX, axis=values.ndim - 1)
    column = jnp.arange(PIX) % SIDE
    inside = ((column + column_shift >= 0) & (column + column_shift < SIDE)).astype(values.dtype)
    return moved * inside


def reference(inputs, cotangent, weights, gate_logits, routes):
    highest = lax.Precision.HIGHEST
    gate_values = jax.nn.sigmoid(gate_logits)
    w_table = weights.astype(jnp.float32).reshape(EXPERTS, GROUPS, CG, CG, 9)

    def per_sample(grad_total, sample_data):
        x_sample, dy_sample, route_ids, sample_gates = sample_data
        x_patches = x_sample.astype(jnp.float32).reshape(GROUPS, CG, NPATCH, PIX).transpose(2, 0, 1, 3)
        dy_patches = dy_sample.astype(jnp.float32).reshape(GROUPS, CG, NPATCH, PIX).transpose(2, 0, 1, 3)
        dx_total = jnp.zeros(x_patches.shape, jnp.float32)
        dot_list = []
        for rank_index in range(TOPK):
            kernels = w_table[route_ids[:, rank_index]]
            expert_image = jnp.zeros(x_patches.shape, jnp.float32)
            adjoint = jnp.zeros(x_patches.shape, jnp.float32)
            tap_grads = []
            for offset in range(9):
                row_shift = offset // 3 - 1
                column_shift = offset % 3 - 1
                tap_kernel = kernels[..., offset]
                moved_x = shifted(x_patches, row_shift, column_shift)
                expert_image = expert_image + jnp.einsum("ngoi,ngip->ngop", tap_kernel, moved_x, precision=highest)
                adjoint = adjoint + jnp.einsum("ngoi,ngop->ngip", tap_kernel, shifted(dy_patches, -row_shift, -column_shift), precision=highest)
                tap_grads.append(jnp.einsum("ngop,ngip->ngoi", dy_patches, moved_x, precision=highest))
            block_dots = jnp.sum((dy_patches * expert_image).reshape(NPATCH, N_BATCH, -1), axis=2)
            block_dots = lax.optimization_barrier(block_dots.astype(jnp.bfloat16)).astype(jnp.float32)
            dot_list.append(jnp.sum(block_dots, axis=1))
            route_gate = sample_gates[:, rank_index]
            gated_term = (route_gate[:, None, None, None] * adjoint).astype(jnp.bfloat16)
            dx_total = dx_total + lax.optimization_barrier(gated_term).astype(jnp.float32)
            route_grad = jnp.stack(tap_grads, axis=-1) * route_gate[:, None, None, None, None]
            grad_total = grad_total.at[route_ids[:, rank_index]].add(route_grad)
        dx_sample = dx_total.transpose(1, 2, 0, 3).reshape(C, NPATCH * PIX).astype(jnp.bfloat16)
        route_dots = jnp.stack(dot_list, axis=1)
        gate_grad = sample_gates * (1.0 - sample_gates) * route_dots / SIDE
        return grad_total, (dx_sample, gate_grad)

    zero_grads = jnp.zeros((EXPERTS, GROUPS, CG, CG, 9), jnp.float32)
    grad_total, (d_inputs, gate_grad) = lax.scan(per_sample, zero_grads, (inputs, cotangent, routes, gate_values))
    d_weights = (grad_total / SIDE).reshape(EXPERTS, GROUPS, CG * CG * 9)
    return d_inputs, d_weights, gate_grad
```

```python
import functools

import jax
import jax.numpy as jnp
from jax import lax
from jax.experimental import pallas as pl
from jax.experimental.pallas import tpu as pltpu
from jax.sharding import PartitionSpec as P

MESH = pl.DeviceIdType.MESH
CG = 32
SIDE = 16
PIX = SIDE * SIDE
TAPS = 9
EXP = 8
TOP = 2
NSUB = 4
ES = EXP // NSUB
UR = 80
BF = jnp.bfloat16
F32 = jnp.float32
Z_SIZE = 16


def step_kernel(
    ny, nz, nb, pcol,
    x_hbm, dy_hbm, w_ref, tab_ref, rows_ref, gate_ref, gatev_ref,
    dx_hbm, dw_hbm, gg_ref,
    xg, dyg, taps_buf, wg, ws, wr, gb, gs, gr, rr, rs, dxs, parts, dots_s, dots_r, dw_v,
    tap_mask, tail_mask, tail_mask_bf, block,
    act_send, act_recv, act_loc, ag_send, ag_recv, wy_send, wy_recv, gy_send, gy_recv,
    rs_send, rs_recv, dx_send, dx_recv, dot_send, dot_recv, out_sem,
):
    half = nz // 2
    nx = nb // 2
    patches = nb * pcol
    ticks = half * NSUB
    grid_id = lax.axis_index("grid")
    b = lax.axis_index("batch")
    y = lax.div(grid_id, nz)
    z = lax.rem(grid_id, nz)
    xi = lax.div(b, 2)
    core = lax.rem(b, 2)
    right = y * nz + lax.rem(z + 1, nz)
    left = y * nz + lax.rem(z + nz - 1, nz)
    hop_to = (right, left)

    def split(j):
        q = lax.div(j, 2)
        far = q + lax.div(q, 2) * (1 - 2 * lax.rem(q, 2))
        return far, lax.rem(j, 2)

    def sender_of(j):
        far, other = split(j)
        return lax.rem(xi + nx - far, nx) * 2 + lax.rem(core + other, 2)

    def receiver_of(j):
        far, other = split(j)
        return lax.rem(xi + far, nx) * 2 + lax.rem(core + other, 2)

    def tile_at(d):
        return lax.rem(y + d, ny)

    barrier = pltpu.get_barrier_semaphore()
    peers = [(right, b), (left, b)]
    peers += [(tile_at(d) * nz + z, b) for d in range(1, ny)]
    peers += [(grid_id, receiver_of(jnp.int32(j))) for j in range(1, nb)]
    for peer in peers:
        pl.semaphore_signal(barrier, inc=1, device_id=peer, device_id_type=MESH)
    pl.semaphore_wait(barrier, len(peers))

    def act_copy(which, j):
        src, dst = ((dy_hbm, dyg), (x_hbm, xg))[which]
        peer = receiver_of(j)
        return pltpu.make_async_remote_copy(
            src_ref=src.at[0, pl.ds(pl.multiple_of(peer * CG, CG), CG), :],
            dst_ref=dst.at[b],
            send_sem=act_send.at[which, j],
            recv_sem=act_recv.at[which, j],
            device_id=(grid_id, peer),
            device_id_type=MESH,
        )

    def act_local(which):
        src, dst = ((dy_hbm, dyg), (x_hbm, xg))[which]
        return pltpu.make_async_copy(
            src.at[0, pl.ds(pl.multiple_of(b * CG, CG), CG), :], dst.at[b], act_loc.at[which]
        )

    def ag_copy(way, s, c, first):
        origin = lax.rem(z + nz - (s - 1), nz) if way == 0 else lax.rem(z + (s - 1), nz)
        piece = pl.ds(c * ES, ES)
        return pltpu.make_async_remote_copy(
            src_ref=w_ref.at[piece] if first else wg.at[origin, piece],
            dst_ref=wg.at[origin, piece],
            send_sem=ag_send.at[way, s - 1, c],
            recv_sem=ag_recv.at[way, s - 1, c],
            device_id=(hop_to[way], b),
            device_id_type=MESH,
        )

    def wy_copy(d, rel):
        zo = lax.rem(z + rel, nz)
        return pltpu.make_async_remote_copy(
            src_ref=ws.at[d - 1, rel],
            dst_ref=wr.at[y, zo],
            send_sem=wy_send.at[d - 1, rel],
            recv_sem=wy_recv.at[d - 1, rel],
            device_id=(tile_at(d) * nz + z, b),
            device_id_type=MESH,
        )

    def gy_copy(d, rel):
        return pltpu.make_async_remote_copy(
            src_ref=gs.at[d - 1, rel],
            dst_ref=gr.at[d, rel],
            send_sem=gy_send.at[d - 1, rel],
            recv_sem=gy_recv.at[d - 1, rel],
            device_id=(tile_at(d) * nz + z, b),
            device_id_type=MESH,
        )

    def rs_copy(way, t, c):
        return pltpu.make_async_remote_copy(
            src_ref=rs.at[way, t, c],
            dst_ref=rr.at[way, t, c],
            send_sem=rs_send.at[way, t, c],
            recv_sem=rs_recv.at[way, t, c],
            device_id=(hop_to[way], b),
            device_id_type=MESH,
        )

    def dx_copy(j):
        s = sender_of(j)
        return pltpu.make_async_remote_copy(
            src_ref=dxs.at[s],
            dst_ref=dx_hbm.at[0, pl.ds(pl.multiple_of(b * CG, CG), CG), :],
            send_sem=dx_send.at[j],
            recv_sem=dx_recv.at[j],
            device_id=(grid_id, s),
            device_id_type=MESH,
        )

    def dot_copy(j):
        return pltpu.make_async_remote_copy(
            src_ref=dots_s,
            dst_ref=dots_r.at[j],
            send_sem=dot_send.at[j],
            recv_sem=dot_recv.at[j],
            device_id=(grid_id, receiver_of(j)),
            device_id_type=MESH,
        )

    act_local(0).start()
    act_local(1).start()
    for way in (0, 1):
        for c in range(NSUB):
            if half > 1 or (c < NSUB // 2) == (way == 0):
                ag_copy(way, 1, c, True).start()
    for j in range(1, nb):
        act_copy(0, jnp.int32(j)).start()
        act_copy(1, jnp.int32(j)).start()

    lane = lax.broadcasted_iota(jnp.int32, (8, PIX), 1)
    column = lax.rem(lane, SIDE)
    row = lax.div(lane, SIDE)
    for t in range(TAPS):
        down, over = t // 3 - 1, t % 3 - 1
        inside = (row - down >= 0) & (row - down < SIDE) & (column - over >= 0) & (column - over < SIDE)
        tap_mask[t] = jnp.where(inside, 1.0, 0.0).astype(F32)
    tail_row = lax.div(lax.broadcasted_iota(jnp.int32, (CG, 128), 0), 16)
    tail_lane = lax.div(lax.broadcasted_iota(jnp.int32, (CG, 128), 1), CG)
    tail = jnp.where(tail_row == tail_lane, 1.0, 0.0).astype(F32)
    tail_mask[...] = tail
    tail_mask_bf[...] = tail.astype(BF)
    parts[...] = jnp.zeros_like(parts)
    for c in range(NSUB):
        rr[1 if c < NSUB // 2 else 0, 0, c] = jnp.zeros((ES, UR, 128), BF)

    def expert_of(tile, zo):
        return lax.rem(tab_ref[tile, y * nz + zo], EXP)

    def pick(rel):
        zo = lax.rem(z + rel, nz)
        block[...] = wg[zo]
        wr[y, zo] = block[expert_of(y, zo)]
        for d in range(1, ny):
            ws[d - 1, rel] = block[expert_of(tile_at(d), zo)]

    def send_picks(rel):
        for d in range(1, ny):
            wy_copy(d, rel).start()

    def patch_lanes(p):
        return pl.ds(pl.multiple_of(p * PIX, PIX), PIX)

    def grad_patch(j, p):
        s = sender_of(j)
        index = s * pcol + p
        dy = dyg[s, :, patch_lanes(p)].astype(F32).reshape(CG // 8, 8, PIX)
        for t in range(TAPS):
            shift = ((t // 3 - 1) * SIDE + (t % 3 - 1)) % PIX
            moved = dy if shift == 0 else pltpu.roll(dy, shift, 2) * tap_mask[t][None]
            moved = moved.reshape(CG, PIX).astype(BF)
            if t < TAPS - 1:
                taps_buf[index, t * CG : (t + 1) * CG, :] = moved
            else:
                for k in range(4):
                    taps_buf[index, (t + k) * CG : (t + k + 1) * CG, :] = moved
        xp = xg[s, :, patch_lanes(p)]
        dims = (((1,), (1,)), ((), ()))
        main = lax.dot_general(xp, taps_buf[index, : 8 * CG, :], dims, preferred_element_type=F32)
        last = lax.dot_general(xp, taps_buf[index, 8 * CG :, :], dims, preferred_element_type=F32)
        last = last * tail_mask[...]
        gb[index, 0:32, :] = main[:, :128]
        gb[index, 32:64, :] = main[:, 128:]
        gb[index, 64:80, :] = last[:16] + last[16:]

    def grad_stage(rel):
        zo = lax.rem(z + rel, nz)
        for d in range(ny):
            route = lax.div(tab_ref[y, tile_at(d) * nz + zo], EXP)
            value = (gb[lax.div(route, TOP)] * gate_ref[0, route]).astype(BF)
            if d == 0:
                gr[0, rel] = value
            else:
                gs[d - 1, rel] = value

    def route_unit(route):
        owner = lax.div(rows_ref[y, route], EXP)
        return wr[lax.div(owner, nz), lax.rem(owner, nz)]

    def dx_patch(j, p):
        s = sender_of(j)
        index = s * pcol + p
        mains, tails = [], []
        for k in range(TOP):
            unit = route_unit(index * TOP + k)
            mains.append(jnp.concatenate([unit[0:32], unit[32:64]], axis=1))
            tails.append(jnp.concatenate([unit[64:80], unit[64:80]], axis=0) * tail_mask_bf[...])
        adjoint = jnp.dot(
            jnp.concatenate(mains, axis=0), taps_buf[index, : 8 * CG, :], preferred_element_type=F32
        ) + jnp.dot(
            jnp.concatenate(tails, axis=0), taps_buf[index, 8 * CG :, :], preferred_element_type=F32
        )
        xp = xg[s, :, patch_lanes(p)].astype(F32)
        total = jnp.zeros((CG, PIX), F32)
        for k in range(TOP):
            one = adjoint[k * CG : (k + 1) * CG]
            prod = xp * one
            prod = (prod[0:8] + prod[8:16]) + (prod[16:24] + prod[24:32])
            prod = prod[:, :128] + prod[:, 128:]
            parts[pl.ds(index * TOP + k, 1), :] = jnp.sum(prod, axis=0, keepdims=True)
            total = total + (gate_ref[0, index * TOP + k] * one).astype(BF).astype(F32)
        dxs[s, :, patch_lanes(p)] = total.astype(BF)

    def own_part(rel, e):
        zo = lax.rem(z + rel, nz)
        total = None
        for d in range(ny):
            tile = lax.rem(y + ny - d, ny)
            hit = jnp.where(expert_of(tile, zo) == e, 1.0, 0.0).astype(F32)
            term = gr[d, rel].astype(F32) * hit
            total = term if total is None else total + term
        return total

    def rs_add(way, t, c, fresh):
        rel = half - t if way == 0 else nz - half + t
        for k in range(ES):
            value = own_part(rel, c * ES + k)
            if not fresh:
                value = value + rr[way, t - 1, c, k].astype(F32)
            rs[way, t, c, k] = value.astype(BF)

    def wait_grads(rel):
        for d in range(1, ny):
            gy_copy(d, rel).wait_recv()

    wg[z] = w_ref[...]
    pick(jnp.int32(0))

    def phase_one(k, carry):
        s = lax.div(k, NSUB) + 1
        c = lax.rem(k, NSUB)
        low = c < NSUB // 2
        for way in (0, 1):
            mine = low if way == 0 else jnp.logical_not(low)

            @pl.when(jnp.logical_or(s < half, mine))
            def _():
                ag_copy(way, s, c, False).wait_recv()

            @pl.when(jnp.logical_or(s + 1 < half, jnp.logical_and(s + 1 == half, mine)))
            def _():
                ag_copy(way, s + 1, c, False).start()

        @pl.when(c == 0)
        def _():
            send_picks(s - 1)

            @pl.when(s > 1)
            def _():
                send_picks(nz - s + 1)

        @pl.when(k < patches)
        def _():
            j = lax.div(k, pcol)

            @pl.when(lax.rem(k, pcol) == 0)
            def _():
                @pl.when(j == 0)
                def _():
                    act_local(0).wait()
                    act_local(1).wait()

                @pl.when(j > 0)
                def _():
                    act_copy(0, j).wait_recv()
                    act_copy(1, j).wait_recv()

            grad_patch(j, lax.rem(k, pcol))

        @pl.when(c == NSUB - 1)
        def _():
            pick(s)

            @pl.when(s < half)
            def _():
                pick(nz - s)

        return carry

    lax.fori_loop(0, ticks, phase_one, 0)

    def stage_one(i, carry):
        rel = lax.rem(half + lax.div(i + 1, 2) * (1 - 2 * lax.rem(i, 2)) + nz, nz)
        grad_stage(rel)
        return carry

    def stage_two(i, carry):
        rel = lax.rem(half + lax.div(i + 1, 2) * (1 - 2 * lax.rem(i, 2)) + nz, nz)
        for d in range(1, ny):
            gy_copy(d, rel).start()
        return carry

    send_picks(jnp.int32(half))
    lax.fori_loop(0, nz, stage_one, 0)
    lax.fori_loop(0, nz, stage_two, 0)

    def wait_kernels(rel, carry):
        for d in range(1, ny):
            wy_copy(d, rel).wait_recv()
        return carry

    lax.fori_loop(0, nz, wait_kernels, 0)

    wait_grads(jnp.int32(half))
    for c in range(NSUB):
        rs_add(0 if c < NSUB // 2 else 1, 0, c, True)

    def dx_tick(k):
        i = k - 1
        j = nb - 1 - lax.div(i, pcol)

        @pl.when(jnp.logical_and(i >= 0, i < patches))
        def _():
            dx_patch(j, lax.rem(i, pcol))

        return i

    def dx_flush(k):
        done = k - 2

        @pl.when(jnp.logical_and(done >= 0, jnp.logical_and(done < patches, lax.rem(done, pcol) == pcol - 1)))
        def _():
            j = nb - 1 - lax.div(done, pcol)

            @pl.when(j > 0)
            def _():
                dx_copy(j).start()

    dx_tick(jnp.int32(1))
    for c in range(NSUB):
        rs_copy(0 if c < NSUB // 2 else 1, 0, c).start()

    def phase_two(k, carry):
        t = lax.div(k, NSUB)
        c = lax.rem(k, NSUB)
        low = c < NSUB // 2

        @pl.when(c == 0)
        def _():
            wait_grads(half - t)
            wait_grads(nz - half + t)

        for way in (0, 1):
            mine = low if way == 0 else jnp.logical_not(low)

            @pl.when(jnp.logical_or(t > 1, mine))
            def _():
                rs_copy(way, t - 1, c).wait_recv()

            rs_add(way, t, c, False)
        dx_flush(k - NSUB + 2)
        dx_tick(k - NSUB + 2)
        for way in (0, 1):
            rs_copy(way, t, c).start()
        return carry

    lax.fori_loop(NSUB, ticks, phase_two, 0)
    tail_ticks = range(ticks - NSUB + 2, patches + 3)
    for k in tail_ticks:
        dx_flush(jnp.int32(k))
        dx_tick(jnp.int32(k))

    own_dx = pltpu.make_async_copy(
        dxs.at[b], dx_hbm.at[0, pl.ds(pl.multiple_of(b * CG, CG), CG), :], out_sem.at[0]
    )
    own_dx.start()
    dots = jnp.sum(parts[...].T, axis=0, keepdims=True).astype(BF).astype(F32)
    dots_s[...] = jnp.broadcast_to(dots, (8, 128))

    wait_grads(jnp.int32(0))
    last = half - 1
    for c in range(NSUB):
        for way in (0, 1):
            if half > 1 or (c < NSUB // 2) == (way == 0):
                rs_copy(way, last, c).wait_recv()
        if c == 0:
            for j in range(1, nb):
                dot_copy(jnp.int32(j)).start()
        for k in range(ES):
            value = own_part(jnp.int32(0), c * ES + k)
            value = value + rr[0, last, c, k].astype(F32) + rr[1, last, c, k].astype(F32)
            dw_v[c * ES + k] = value * (1.0 / SIDE)
    out_dw = pltpu.make_async_copy(dw_v, dw_hbm, out_sem.at[1])
    out_dw.start()

    total = dots_s[...]
    for j in range(1, nb):
        dot_copy(jnp.int32(j)).wait_recv()
        total = total + dots_r[j]
    gates = gatev_ref[...]
    gg_ref[...] = gates * (1.0 - gates) * total * (1.0 / SIDE)

    for j in range(1, nb):
        act_copy(0, jnp.int32(j)).wait_send()
        act_copy(1, jnp.int32(j)).wait_send()
        dot_copy(jnp.int32(j)).wait_send()
        dx_copy(jnp.int32(j)).wait_send()
        dx_copy(jnp.int32(j)).wait_recv()

    def drain_ring(k, carry):
        s = lax.div(k, NSUB)
        c = lax.rem(k, NSUB)
        low = c < NSUB // 2
        for way in (0, 1):
            mine = low if way == 0 else jnp.logical_not(low)

            @pl.when(jnp.logical_or(s + 1 < half, mine))
            def _():
                ag_copy(way, s + 1, c, False).wait_send()

            @pl.when(jnp.logical_or(s > 0, mine))
            def _():
                rs_copy(way, s, c).wait_send()

        return carry

    lax.fori_loop(0, ticks, drain_ring, 0)

    def drain_rows(rel, carry):
        for d in range(1, ny):
            wy_copy(d, rel).wait_send()
            gy_copy(d, rel).wait_send()
        return carry

    lax.fori_loop(0, nz, drain_rows, 0)
    own_dx.wait()
    out_dw.wait()


def per_device(nz, inputs, cotangent, weights, gate_logits, routes):
    grid_size = lax.axis_size("grid")
    nb = lax.axis_size("batch")
    ny = grid_size // nz
    half = nz // 2
    _, channels, width = inputs.shape
    pcol = width // PIX
    patches = nb * pcol
    count = patches * TOP
    index = lax.axis_index("grid")
    y, z = index // nz, index % nz

    kernels = weights.reshape(EXP, CG, CG, TAPS)
    main = kernels[..., :8].reshape(EXP, CG, CG, 2, 4).transpose(0, 3, 2, 4, 1).reshape(EXP, 64, 128)
    last = kernels[..., 8].reshape(EXP, CG, 2, 16).transpose(0, 3, 2, 1).reshape(EXP, 16, 64)
    units = jnp.concatenate([main, jnp.pad(last, ((0, 0), (0, 0), (0, 64)))], axis=1)

    near = routes.reshape(nb, ny, nz, pcol, TOP)
    near = lax.dynamic_index_in_dim(near, z, 2, keepdims=False)
    rows = near.transpose(1, 0, 2, 3).reshape(ny, count)
    code = jnp.arange(count, dtype=jnp.int32)[None, :] * EXP + rows % EXP
    named = (rows // EXP)[:, None, :] == jnp.arange(grid_size, dtype=jnp.int32)[None, :, None]
    table = jnp.sum(jnp.where(named, code[:, None, :], 0), axis=2)
    own = lax.dynamic_slice_in_dim(gate_logits, index * pcol, pcol, 1).reshape(1, count)
    gates = jax.nn.sigmoid(own)
    gates = jnp.pad(gates, ((0, 0), (0, 128 - count)))

    vmem, smem, hbm = (
        pl.BlockSpec(memory_space=pltpu.VMEM),
        pl.BlockSpec(memory_space=pltpu.SMEM),
        pl.BlockSpec(memory_space=pl.ANY),
    )
    dma = pltpu.SemaphoreType.DMA
    d_inputs, d_units, grads = pl.pallas_call(
        functools.partial(step_kernel, ny, nz, nb, pcol),
        out_shape=(
            jax.ShapeDtypeStruct(inputs.shape, BF),
            jax.ShapeDtypeStruct((EXP, UR, 128), F32),
            jax.ShapeDtypeStruct((8, 128), F32),
        ),
        in_specs=[hbm, hbm, vmem, smem, smem, smem, vmem],
        out_specs=(hbm, hbm, vmem),
        scratch_shapes=[
            pltpu.VMEM((nb, CG, width), BF),
            pltpu.VMEM((nb, CG, width), BF),
            pltpu.VMEM((patches, 12 * CG, PIX), BF),
            pltpu.VMEM((nz, EXP, UR, 128), BF),
            pltpu.VMEM((ny - 1, nz, UR, 128), BF),
            pltpu.VMEM((ny, nz, UR, 128), BF),
            pltpu.VMEM((patches, UR, 128), F32),
            pltpu.VMEM((ny - 1, nz, UR, 128), BF),
            pltpu.VMEM((ny, nz, UR, 128), BF),
            pltpu.VMEM((2, half, NSUB, ES, UR, 128), BF),
            pltpu.VMEM((2, half, NSUB, ES, UR, 128), BF),
            pltpu.VMEM((nb, CG, width), BF),
            pltpu.VMEM((128, 128), F32),
            pltpu.VMEM((8, 128), F32),
            pltpu.VMEM((nb, 8, 128), F32),
            pltpu.VMEM((EXP, UR, 128), F32),
            pltpu.VMEM((TAPS, 8, PIX), F32),
            pltpu.VMEM((CG, 128), F32),
            pltpu.VMEM((CG, 128), BF),
            pltpu.VMEM((EXP, UR, 128), BF),
            dma((2, nb)), dma((2, nb)), dma((2,)),
            dma((2, half, NSUB)), dma((2, half, NSUB)),
            dma((ny - 1, nz)), dma((ny - 1, nz)),
            dma((ny - 1, nz)), dma((ny - 1, nz)),
            dma((2, half, NSUB)), dma((2, half, NSUB)),
            dma((nb,)), dma((nb,)), dma((nb,)), dma((nb,)), dma((2,)),
        ],
        compiler_params=pltpu.CompilerParams(collective_id=0, has_side_effects=True),
        name="expert_step",
    )(inputs, cotangent, units, table, rows, gates, jnp.broadcast_to(gates, (8, 128)))

    main = d_units[:, :64].reshape(EXP, 2, CG, 4, CG).transpose(0, 4, 2, 1, 3).reshape(EXP, CG, CG, 8)
    last = d_units[:, 64:, :64].reshape(EXP, 16, 2, CG).transpose(0, 3, 2, 1).reshape(EXP, CG, CG, 1)
    d_weights = jnp.concatenate([main, last], axis=3).reshape(weights.shape)
    gate_grad = grads[0, :count].reshape(nb, pcol, TOP)
    return (d_inputs, d_weights, gate_grad)


def solution(mesh):
    grid_size = mesh.shape["grid"]
    nz = Z_SIZE if grid_size % Z_SIZE == 0 else grid_size // 2
    placed = (
        P("batch", None, "grid"),
        P("batch", None, "grid"),
        P("grid", "batch", None),
        P(),
        P(),
    )
    return jax.shard_map(
        functools.partial(per_device, nz),
        mesh=mesh,
        in_specs=placed,
        out_specs=(P("batch", None, "grid"), P("grid", "batch", None), P(None, "grid", None)),
        check_vma=False,
    )
```

```python
import functools

import jax
import jax.numpy as jnp
from jax import lax
from jax.experimental import pallas as pl
from jax.experimental.pallas import tpu as pltpu
from jax.sharding import PartitionSpec as P

MESH = pl.DeviceIdType.MESH
CG = 32
SIDE = 16
PIX = SIDE * SIDE
TAPS = 9
ROW = CG * TAPS
EXP = 8
TOP = 2
NSUB = 4
ES = EXP // NSUB
UR = 80
BF = jnp.bfloat16
F32 = jnp.float32
Z_SIZE = 16


def step_kernel(
    ny, nz, nb, pcol,
    x_hbm, dy_hbm, w_ref, tab_ref, rows_ref, logit_ref,
    dx_hbm, dw_hbm, gg_ref,
    xg, dyg, taps_buf, wg, ws, wr, gb, gs, gr, rr, rs, dxs, parts, dots_s, dots_r, dw_v,
    tap_mask, tail_mask, tail_mask_bf, block, wl, flat_a, flat_t, out_v, gate_rows,
    act_send, act_recv, act_loc, ag_send, ag_recv, wy_send, wy_recv, gy_send, gy_recv,
    rs_send, rs_recv, dx_send, dx_recv, dot_send, dot_recv, out_sem,
):
    half = nz // 2
    nx = nb // 2
    patches = nb * pcol
    ticks = half * NSUB
    grid_id = lax.axis_index("grid")
    b = lax.axis_index("batch")
    y = lax.div(grid_id, nz)
    z = lax.rem(grid_id, nz)
    xi = lax.div(b, 2)
    core = lax.rem(b, 2)
    right = y * nz + lax.rem(z + 1, nz)
    left = y * nz + lax.rem(z + nz - 1, nz)
    hop_to = (right, left)

    def split(j):
        q = lax.div(j, 2)
        far = q + lax.div(q, 2) * (1 - 2 * lax.rem(q, 2))
        return far, lax.rem(j, 2)

    def sender_of(j):
        far, other = split(j)
        return lax.rem(xi + nx - far, nx) * 2 + lax.rem(core + other, 2)

    def receiver_of(j):
        far, other = split(j)
        return lax.rem(xi + far, nx) * 2 + lax.rem(core + other, 2)

    def tile_at(d):
        return lax.rem(y + d, ny)

    barrier = pltpu.get_barrier_semaphore()
    peers = [(right, b), (left, b)]
    peers += [(tile_at(d) * nz + z, b) for d in range(1, ny)]
    peers += [(grid_id, receiver_of(jnp.int32(j))) for j in range(1, nb)]
    for peer in peers:
        pl.semaphore_signal(barrier, inc=1, device_id=peer, device_id_type=MESH)

    quarter = lax.div(lax.broadcasted_iota(jnp.int32, (CG, 128), 1), CG)
    lane8 = lax.broadcasted_iota(jnp.int32, (8, 128), 1)
    for oh in range(8):
        flat = w_ref[:, oh * 4 * ROW : (oh + 1) * 4 * ROW].astype(F32)
        for ol in range(4):
            for t in range(3):
                at = (2 * ol + t) * 128
                piece = flat[:, at : at + 128]
                if ol:
                    piece = pltpu.roll(piece, 128 - CG * ol, 1)
                    if t < 2:
                        after = pltpu.roll(flat[:, at + 128 : at + 256], 128 - CG * ol, 1)
                        piece = jnp.where(lane8 < 128 - CG * ol, piece, after)
                flat_a[t, pl.ds(oh * 4 + ol, EXP, stride=CG), :] = piece
    for h in range(2):
        for t in range(3):
            flat_t[h, t * 128 : (t + 1) * 128, :] = flat_a[t, h * 128 : (h + 1) * 128, :].T

    def turned(value):
        return [value] + [pltpu.roll(value, CG * k, 1) for k in range(1, 4)]

    for h in range(2):
        for th in range(2):
            turns = [turned(flat_t[h, pl.ds(th * 4 + tl, CG, stride=TAPS), :]) for tl in range(4)]
            for el in range(4):
                unit = turns[0][-el % 4]
                for tl in range(1, 4):
                    unit = jnp.where(quarter == tl, turns[tl][(tl - el) % 4], unit)
                wl[4 * h + el, th * CG : (th + 1) * CG, :] = unit.astype(BF)
        turns = turned(flat_t[h, pl.ds(8, CG, stride=TAPS), :])
        for el in range(4):
            low, high = turns[-el % 4][:16], turns[(1 - el) % 4][16:]
            unit = jnp.where(quarter[:16] == 0, low, jnp.where(quarter[:16] == 1, high, 0.0))
            wl[4 * h + el, 64:80, :] = unit.astype(BF)

    gates = jax.nn.sigmoid(logit_ref[...])
    gate_rows[...] = jnp.broadcast_to(gates, (128, 128)).T
    pl.semaphore_wait(barrier, len(peers))

    def act_copy(which, j):
        src, dst = ((dy_hbm, dyg), (x_hbm, xg))[which]
        peer = receiver_of(j)
        return pltpu.make_async_remote_copy(
            src_ref=src.at[0, pl.ds(pl.multiple_of(peer * CG, CG), CG), :],
            dst_ref=dst.at[b],
            send_sem=act_send.at[which, j],
            recv_sem=act_recv.at[which, j],
            device_id=(grid_id, peer),
            device_id_type=MESH,
        )

    def act_local(which):
        src, dst = ((dy_hbm, dyg), (x_hbm, xg))[which]
        return pltpu.make_async_copy(
            src.at[0, pl.ds(pl.multiple_of(b * CG, CG), CG), :], dst.at[b], act_loc.at[which]
        )

    def ag_copy(way, s, c, first):
        origin = lax.rem(z + nz - (s - 1), nz) if way == 0 else lax.rem(z + (s - 1), nz)
        piece = pl.ds(c * ES, ES)
        return pltpu.make_async_remote_copy(
            src_ref=wl.at[piece] if first else wg.at[origin, piece],
            dst_ref=wg.at[origin, piece],
            send_sem=ag_send.at[way, s - 1, c],
            recv_sem=ag_recv.at[way, s - 1, c],
            device_id=(hop_to[way], b),
            device_id_type=MESH,
        )

    def wy_copy(d, rel):
        zo = lax.rem(z + rel, nz)
        return pltpu.make_async_remote_copy(
            src_ref=ws.at[d - 1, rel],
            dst_ref=wr.at[y, zo],
            send_sem=wy_send.at[d - 1, rel],
            recv_sem=wy_recv.at[d - 1, rel],
            device_id=(tile_at(d) * nz + z, b),
            device_id_type=MESH,
        )

    def gy_copy(d, rel):
        return pltpu.make_async_remote_copy(
            src_ref=gs.at[d - 1, rel],
            dst_ref=gr.at[d, rel],
            send_sem=gy_send.at[d - 1, rel],
            recv_sem=gy_recv.at[d - 1, rel],
            device_id=(tile_at(d) * nz + z, b),
            device_id_type=MESH,
        )

    def rs_copy(way, t, c):
        return pltpu.make_async_remote_copy(
            src_ref=rs.at[way, t, c],
            dst_ref=rr.at[way, t, c],
            send_sem=rs_send.at[way, t, c],
            recv_sem=rs_recv.at[way, t, c],
            device_id=(hop_to[way], b),
            device_id_type=MESH,
        )

    def dx_copy(j):
        s = sender_of(j)
        return pltpu.make_async_remote_copy(
            src_ref=dxs.at[s],
            dst_ref=dx_hbm.at[0, pl.ds(pl.multiple_of(b * CG, CG), CG), :],
            send_sem=dx_send.at[j],
            recv_sem=dx_recv.at[j],
            device_id=(grid_id, s),
            device_id_type=MESH,
        )

    def dot_copy(j):
        return pltpu.make_async_remote_copy(
            src_ref=dots_s,
            dst_ref=dots_r.at[j],
            send_sem=dot_send.at[j],
            recv_sem=dot_recv.at[j],
            device_id=(grid_id, receiver_of(j)),
            device_id_type=MESH,
        )

    act_local(0).start()
    act_local(1).start()
    for j in range(1, nb):
        act_copy(0, jnp.int32(j)).start()
        act_copy(1, jnp.int32(j)).start()
    for way in (0, 1):
        for c in range(NSUB):
            if half > 1 or (c < NSUB // 2) == (way == 0):
                ag_copy(way, 1, c, True).start()

    lane = lax.broadcasted_iota(jnp.int32, (8, PIX), 1)
    column = lax.rem(lane, SIDE)
    row = lax.div(lane, SIDE)
    for t in range(TAPS):
        down, over = t // 3 - 1, t % 3 - 1
        inside = (row - down >= 0) & (row - down < SIDE) & (column - over >= 0) & (column - over < SIDE)
        tap_mask[t] = jnp.where(inside, 1.0, 0.0).astype(F32)
    tail_row = lax.div(lax.broadcasted_iota(jnp.int32, (CG, 128), 0), 16)
    tail_lane = lax.div(lax.broadcasted_iota(jnp.int32, (CG, 128), 1), CG)
    tail = jnp.where(tail_row == tail_lane, 1.0, 0.0).astype(F32)
    tail_mask[...] = tail
    tail_mask_bf[...] = tail.astype(BF)
    parts[...] = jnp.zeros_like(parts)
    for c in range(NSUB):
        rr[1 if c < NSUB // 2 else 0, 0, c] = jnp.zeros((ES, UR, 128), BF)

    def expert_of(tile, zo):
        return lax.rem(tab_ref[tile, y * nz + zo], EXP)

    def pick(rel):
        zo = lax.rem(z + rel, nz)
        block[...] = wg[zo]
        wr[y, zo] = block[expert_of(y, zo)]
        for d in range(1, ny):
            ws[d - 1, rel] = block[expert_of(tile_at(d), zo)]

    def send_picks(rel):
        for d in range(1, ny):
            wy_copy(d, rel).start()

    def patch_lanes(p):
        return pl.ds(pl.multiple_of(p * PIX, PIX), PIX)

    def grad_patch(j, p):
        s = sender_of(j)
        index = s * pcol + p
        dy = dyg[s, :, patch_lanes(p)].astype(F32).reshape(CG // 8, 8, PIX)
        for t in range(TAPS):
            shift = ((t // 3 - 1) * SIDE + (t % 3 - 1)) % PIX
            moved = dy if shift == 0 else pltpu.roll(dy, shift, 2) * tap_mask[t][None]
            moved = moved.reshape(CG, PIX).astype(BF)
            if t < TAPS - 1:
                taps_buf[index, t * CG : (t + 1) * CG, :] = moved
            else:
                for k in range(4):
                    taps_buf[index, (t + k) * CG : (t + k + 1) * CG, :] = moved
        xp = xg[s, :, patch_lanes(p)]
        dims = (((1,), (1,)), ((), ()))
        main = lax.dot_general(xp, taps_buf[index, : 8 * CG, :], dims, preferred_element_type=F32)
        last = lax.dot_general(xp, taps_buf[index, 8 * CG :, :], dims, preferred_element_type=F32)
        last = last * tail_mask[...]
        gb[index, 0:32, :] = main[:, :128]
        gb[index, 32:64, :] = main[:, 128:]
        gb[index, 64:80, :] = last[:16] + last[16:]

    def grad_stage(rel):
        zo = lax.rem(z + rel, nz)
        for d in range(ny):
            route = lax.div(tab_ref[y, tile_at(d) * nz + zo], EXP)
            value = (gb[lax.div(route, TOP)] * gate_rows[pl.ds(route, 1), :]).astype(BF)
            if d == 0:
                gr[0, rel] = value
            else:
                gs[d - 1, rel] = value

    def route_unit(route):
        owner = lax.div(rows_ref[y, route], EXP)
        return wr[lax.div(owner, nz), lax.rem(owner, nz)]

    def dx_patch(j, p):
        s = sender_of(j)
        index = s * pcol + p
        mains, tails = [], []
        for k in range(TOP):
            unit = route_unit(index * TOP + k)
            mains.append(jnp.concatenate([unit[0:32], unit[32:64]], axis=1))
            tails.append(jnp.concatenate([unit[64:80], unit[64:80]], axis=0) * tail_mask_bf[...])
        adjoint = jnp.dot(
            jnp.concatenate(mains, axis=0), taps_buf[index, : 8 * CG, :], preferred_element_type=F32
        ) + jnp.dot(
            jnp.concatenate(tails, axis=0), taps_buf[index, 8 * CG :, :], preferred_element_type=F32
        )
        xp = xg[s, :, patch_lanes(p)].astype(F32)
        total = jnp.zeros((CG, PIX), F32)
        for k in range(TOP):
            one = adjoint[k * CG : (k + 1) * CG]
            prod = xp * one
            prod = (prod[0:8] + prod[8:16]) + (prod[16:24] + prod[24:32])
            prod = prod[:, :128] + prod[:, 128:]
            parts[pl.ds(index * TOP + k, 1), :] = jnp.sum(prod, axis=0, keepdims=True)
            gate = gate_rows[pl.ds(index * TOP + k, 1), :]
            gate = jnp.concatenate([gate, gate], axis=1)
            total = total + (gate * one).astype(BF).astype(F32)
        dxs[s, :, patch_lanes(p)] = total.astype(BF)

    def own_part(rel, e):
        zo = lax.rem(z + rel, nz)
        total = None
        for d in range(ny):
            tile = lax.rem(y + ny - d, ny)
            hit = jnp.where(expert_of(tile, zo) == e, 1.0, 0.0).astype(F32)
            term = gr[d, rel].astype(F32) * hit
            total = term if total is None else total + term
        return total

    def rs_add(way, t, c, fresh):
        rel = half - t if way == 0 else nz - half + t
        for k in range(ES):
            value = own_part(rel, c * ES + k)
            if not fresh:
                value = value + rr[way, t - 1, c, k].astype(F32)
            rs[way, t, c, k] = value.astype(BF)

    def wait_grads(rel):
        for d in range(1, ny):
            gy_copy(d, rel).wait_recv()

    wg[z] = wl[...]
    pick(jnp.int32(0))

    def phase_one(k, carry):
        s = lax.div(k, NSUB) + 1
        c = lax.rem(k, NSUB)
        low = c < NSUB // 2
        for way in (0, 1):
            mine = low if way == 0 else jnp.logical_not(low)

            @pl.when(jnp.logical_or(s < half, mine))
            def _():
                ag_copy(way, s, c, False).wait_recv()

            @pl.when(jnp.logical_or(s + 1 < half, jnp.logical_and(s + 1 == half, mine)))
            def _():
                ag_copy(way, s + 1, c, False).start()

        @pl.when(c == 0)
        def _():
            send_picks(s - 1)

            @pl.when(s > 1)
            def _():
                send_picks(nz - s + 1)

        @pl.when(k < patches)
        def _():
            j = lax.div(k, pcol)

            @pl.when(lax.rem(k, pcol) == 0)
            def _():
                @pl.when(j == 0)
                def _():
                    act_local(0).wait()
                    act_local(1).wait()

                @pl.when(j > 0)
                def _():
                    act_copy(0, j).wait_recv()
                    act_copy(1, j).wait_recv()

            grad_patch(j, lax.rem(k, pcol))

        @pl.when(c == NSUB - 1)
        def _():
            pick(s)

            @pl.when(s < half)
            def _():
                pick(nz - s)

        return carry

    lax.fori_loop(0, ticks, phase_one, 0)

    def stage_one(i, carry):
        rel = lax.rem(half + lax.div(i + 1, 2) * (1 - 2 * lax.rem(i, 2)) + nz, nz)
        grad_stage(rel)
        return carry

    def stage_two(i, carry):
        rel = lax.rem(half + lax.div(i + 1, 2) * (1 - 2 * lax.rem(i, 2)) + nz, nz)
        for d in range(1, ny):
            gy_copy(d, rel).start()
        return carry

    send_picks(jnp.int32(half))
    lax.fori_loop(0, nz, stage_one, 0)
    lax.fori_loop(0, nz, stage_two, 0)

    def wait_kernels(rel, carry):
        for d in range(1, ny):
            wy_copy(d, rel).wait_recv()
        return carry

    lax.fori_loop(0, nz, wait_kernels, 0)

    wait_grads(jnp.int32(half))
    for c in range(NSUB):
        rs_add(0 if c < NSUB // 2 else 1, 0, c, True)

    def dx_tick(k):
        i = k - 1
        j = nb - 1 - lax.div(i, pcol)

        @pl.when(jnp.logical_and(i >= 0, i < patches))
        def _():
            dx_patch(j, lax.rem(i, pcol))

        return i

    def dx_flush(k):
        done = k - 2

        @pl.when(jnp.logical_and(done >= 0, jnp.logical_and(done < patches, lax.rem(done, pcol) == pcol - 1)))
        def _():
            j = nb - 1 - lax.div(done, pcol)

            @pl.when(j > 0)
            def _():
                dx_copy(j).start()

    dx_tick(jnp.int32(1))
    for c in range(NSUB):
        rs_copy(0 if c < NSUB // 2 else 1, 0, c).start()

    def phase_two(k, carry):
        t = lax.div(k, NSUB)
        c = lax.rem(k, NSUB)
        low = c < NSUB // 2

        @pl.when(c == 0)
        def _():
            wait_grads(half - t)
            wait_grads(nz - half + t)

        for way in (0, 1):
            mine = low if way == 0 else jnp.logical_not(low)

            @pl.when(jnp.logical_or(t > 1, mine))
            def _():
                rs_copy(way, t - 1, c).wait_recv()

            rs_add(way, t, c, False)
        dx_flush(k - NSUB + 2)
        dx_tick(k - NSUB + 2)
        for way in (0, 1):
            rs_copy(way, t, c).start()
        return carry

    lax.fori_loop(NSUB, ticks, phase_two, 0)
    tail_ticks = range(ticks - NSUB + 2, patches + 3)
    for k in tail_ticks:
        dx_flush(jnp.int32(k))
        dx_tick(jnp.int32(k))

    own_dx = pltpu.make_async_copy(
        dxs.at[b], dx_hbm.at[0, pl.ds(pl.multiple_of(b * CG, CG), CG), :], out_sem.at[0]
    )
    own_dx.start()
    dots = jnp.sum(parts[...].T, axis=0, keepdims=True).astype(BF).astype(F32)
    dots_s[...] = jnp.broadcast_to(dots, (8, 128))

    wait_grads(jnp.int32(0))
    last = half - 1
    for c in range(NSUB):
        for way in (0, 1):
            if half > 1 or (c < NSUB // 2) == (way == 0):
                rs_copy(way, last, c).wait_recv()
        if c == 0:
            for j in range(1, nb):
                dot_copy(jnp.int32(j)).start()
        for k in range(ES):
            value = own_part(jnp.int32(0), c * ES + k)
            value = value + rr[0, last, c, k].astype(F32) + rr[1, last, c, k].astype(F32)
            dw_v[c * ES + k] = value * (1.0 / SIDE)
    for h in range(2):
        for th in range(2):
            turns = [turned(dw_v[4 * h + el, th * CG : (th + 1) * CG, :]) for el in range(4)]
            for tl in range(4):
                value = turns[0][-tl % 4]
                for el in range(1, 4):
                    value = jnp.where(quarter == el, turns[el][(el - tl) % 4], value)
                flat_t[h, pl.ds(th * 4 + tl, CG, stride=TAPS), :] = value
        value = None
        for el in range(4):
            turns = turned(dw_v[4 * h + el, 64:80, :])
            both = jnp.concatenate([turns[el], turns[(el - 1) % 4]], axis=0)
            value = both if value is None else jnp.where(quarter == el, both, value)
        flat_t[h, pl.ds(8, CG, stride=TAPS), :] = value
    for h in range(2):
        for t in range(3):
            flat_a[t, h * 128 : (h + 1) * 128, :] = flat_t[h, t * 128 : (t + 1) * 128, :].T
    lane64 = lax.broadcasted_iota(jnp.int32, (8 * EXP, 128), 1)
    tiles = [None] * TAPS
    for ol in range(4):
        for t in range(3):
            piece = flat_a[t, pl.ds(ol, 8 * EXP, stride=4), :]
            if ol:
                piece = pltpu.roll(piece, CG * ol, 1)
            at = 2 * ol + t
            if t == 2:
                keep = (lane64 >= CG * ol) & (lane64 < CG * (ol + 1))
            else:
                keep = lane64 >= CG * ol
            tiles[at] = jnp.where(keep, piece, 0.0 if tiles[at] is None else tiles[at])
            if ol and t < 2:
                at += 1
                tiles[at] = jnp.where(lane64 < CG * ol, piece, 0.0 if tiles[at] is None else tiles[at])
    for q in range(TAPS):
        out_v[pl.ds(q, 8 * EXP, stride=TAPS), :] = tiles[q]
    out_dw = pltpu.make_async_copy(out_v, dw_hbm, out_sem.at[1])
    out_dw.start()

    total = dots_s[...]
    for j in range(1, nb):
        dot_copy(jnp.int32(j)).wait_recv()
        total = total + dots_r[j]
    gg_ref[...] = gates * (1.0 - gates) * total * (1.0 / SIDE)

    for j in range(1, nb):
        act_copy(0, jnp.int32(j)).wait_send()
        act_copy(1, jnp.int32(j)).wait_send()
        dot_copy(jnp.int32(j)).wait_send()
        dx_copy(jnp.int32(j)).wait_send()
        dx_copy(jnp.int32(j)).wait_recv()

    def drain_ring(k, carry):
        s = lax.div(k, NSUB)
        c = lax.rem(k, NSUB)
        low = c < NSUB // 2
        for way in (0, 1):
            mine = low if way == 0 else jnp.logical_not(low)

            @pl.when(jnp.logical_or(s + 1 < half, mine))
            def _():
                ag_copy(way, s + 1, c, False).wait_send()

            @pl.when(jnp.logical_or(s > 0, mine))
            def _():
                rs_copy(way, s, c).wait_send()

        return carry

    lax.fori_loop(0, ticks, drain_ring, 0)

    def drain_rows(rel, carry):
        for d in range(1, ny):
            wy_copy(d, rel).wait_send()
            gy_copy(d, rel).wait_send()
        return carry

    lax.fori_loop(0, nz, drain_rows, 0)
    own_dx.wait()
    out_dw.wait()


def per_device(nz, inputs, cotangent, weights, gate_logits, routes):
    grid_size = lax.axis_size("grid")
    nb = lax.axis_size("batch")
    ny = grid_size // nz
    half = nz // 2
    _, channels, width = inputs.shape
    pcol = width // PIX
    patches = nb * pcol
    count = patches * TOP
    index = lax.axis_index("grid")
    y, z = index // nz, index % nz

    near = routes.reshape(nb, ny, nz, pcol, TOP)
    near = lax.dynamic_index_in_dim(near, z, 2, keepdims=False)
    rows = near.transpose(1, 0, 2, 3).reshape(ny, count)
    code = jnp.arange(count, dtype=jnp.int32)[None, :] * EXP + rows % EXP
    named = (rows // EXP)[:, None, :] == jnp.arange(grid_size, dtype=jnp.int32)[None, :, None]
    table = jnp.sum(jnp.where(named, code[:, None, :], 0), axis=2)
    own = lax.dynamic_slice_in_dim(gate_logits, index * pcol, pcol, 1).reshape(1, count)
    logits = jnp.pad(own, ((0, 0), (0, 128 - count)))

    vmem, smem, hbm = (
        pl.BlockSpec(memory_space=pltpu.VMEM),
        pl.BlockSpec(memory_space=pltpu.SMEM),
        pl.BlockSpec(memory_space=pl.ANY),
    )
    dma = pltpu.SemaphoreType.DMA
    d_inputs, d_flat, grads = pl.pallas_call(
        functools.partial(step_kernel, ny, nz, nb, pcol),
        out_shape=(
            jax.ShapeDtypeStruct(inputs.shape, BF),
            jax.ShapeDtypeStruct((EXP * ROW // 4, 128), F32),
            jax.ShapeDtypeStruct((8, 128), F32),
        ),
        in_specs=[hbm, hbm, vmem, smem, smem, vmem],
        out_specs=(hbm, hbm, vmem),
        scratch_shapes=[
            pltpu.VMEM((nb, CG, width), BF),
            pltpu.VMEM((nb, CG, width), BF),
            pltpu.VMEM((patches, 12 * CG, PIX), BF),
            pltpu.VMEM((nz, EXP, UR, 128), BF),
            pltpu.VMEM((ny - 1, nz, UR, 128), BF),
            pltpu.VMEM((ny, nz, UR, 128), BF),
            pltpu.VMEM((patches, UR, 128), F32),
            pltpu.VMEM((ny - 1, nz, UR, 128), BF),
            pltpu.VMEM((ny, nz, UR, 128), BF),
            pltpu.VMEM((2, half, NSUB, ES, UR, 128), BF),
            pltpu.VMEM((2, half, NSUB, ES, UR, 128), BF),
            pltpu.VMEM((nb, CG, width), BF),
            pltpu.VMEM((128, 128), F32),
            pltpu.VMEM((8, 128), F32),
            pltpu.VMEM((nb, 8, 128), F32),
            pltpu.VMEM((EXP, UR, 128), F32),
            pltpu.VMEM((TAPS, 8, PIX), F32),
            pltpu.VMEM((CG, 128), F32),
            pltpu.VMEM((CG, 128), BF),
            pltpu.VMEM((EXP, UR, 128), BF),
            pltpu.VMEM((EXP, UR, 128), BF),
            pltpu.VMEM((3, EXP * CG, 128), F32),
            pltpu.VMEM((2, 3 * 128, 128), F32),
            pltpu.VMEM((EXP * ROW // 4, 128), F32),
            pltpu.VMEM((128, 128), F32),
            dma((2, nb)), dma((2, nb)), dma((2,)),
            dma((2, half, NSUB)), dma((2, half, NSUB)),
            dma((ny - 1, nz)), dma((ny - 1, nz)),
            dma((ny - 1, nz)), dma((ny - 1, nz)),
            dma((2, half, NSUB)), dma((2, half, NSUB)),
            dma((nb,)), dma((nb,)), dma((nb,)), dma((nb,)), dma((2,)),
        ],
        compiler_params=pltpu.CompilerParams(collective_id=0, has_side_effects=True),
        name="expert_step",
    )(inputs, cotangent, weights.reshape(EXP, CG * ROW), table, rows, logits)

    d_weights = d_flat.reshape(weights.shape)
    gate_grad = grads[0, :count].reshape(nb, pcol, TOP)
    return (d_inputs, d_weights, gate_grad)


def solution(mesh):
    grid_size = mesh.shape["grid"]
    nz = Z_SIZE if grid_size % Z_SIZE == 0 else grid_size // 2
    placed = (
        P("batch", None, "grid"),
        P("batch", None, "grid"),
        P("grid", "batch", None),
        P(),
        P(),
    )
    return jax.shard_map(
        functools.partial(per_device, nz),
        mesh=mesh,
        in_specs=placed,
        out_specs=(P("batch", None, "grid"), P("grid", "batch", None), P(None, "grid", None)),
        check_vma=False,
    )
```

```python
import functools

import jax
import jax.numpy as jnp
from jax import lax
from jax.experimental import pallas as pl
from jax.experimental.pallas import tpu as pltpu
from jax.sharding import PartitionSpec as P

MESH = pl.DeviceIdType.MESH
CG = 32
SIDE = 16
PIX = SIDE * SIDE
TAPS = 9
ROW = CG * TAPS
EXP = 8
TOP = 2
NSUB = 4
ES = EXP // NSUB
PER_TICK = 2
UR = 80
BF = jnp.bfloat16
F32 = jnp.float32
Z_SIZE = 16


def step_kernel(
    ny, nz, nb, pcol,
    x_hbm, dy_hbm, w_ref, tab_ref, rows_ref, logit_ref,
    dx_hbm, dw_hbm, gg_ref,
    xg, dyg, taps_buf, wg, ws, wr, gb, gs, gr, rr, rs, dxs, parts, dots_s, dots_r, dw_v,
    tap_mask, tail_mask, tail_mask_bf, block, wl, flat_a, flat_t, out_v, gate_rows,
    act_send, act_recv, act_loc, ag_send, ag_recv, wy_send, wy_recv, gy_send, gy_recv,
    rs_send, rs_recv, dx_send, dx_recv, dot_send, dot_recv, out_sem,
):
    half = nz // 2
    nx = nb // 2
    patches = nb * pcol
    ticks = half * NSUB
    grad_from = 1
    stage_from = grad_from + patches // PER_TICK
    stage_ticks = 4 if nz >= 16 else 2
    rs_from = stage_from + stage_ticks + 1
    dx_from = ticks + 4
    all_ticks = rs_from + ticks
    grid_id = lax.axis_index("grid")
    b = lax.axis_index("batch")
    y = lax.div(grid_id, nz)
    z = lax.rem(grid_id, nz)
    xi = lax.div(b, 2)
    core = lax.rem(b, 2)
    right = y * nz + lax.rem(z + 1, nz)
    left = y * nz + lax.rem(z + nz - 1, nz)
    hop_to = (right, left)

    def split(j):
        q = lax.div(j, 2)
        far = q + lax.div(q, 2) * (1 - 2 * lax.rem(q, 2))
        return far, lax.rem(j, 2)

    def sender_of(j):
        far, other = split(j)
        return lax.rem(xi + nx - far, nx) * 2 + lax.rem(core + other, 2)

    def receiver_of(j):
        far, other = split(j)
        return lax.rem(xi + far, nx) * 2 + lax.rem(core + other, 2)

    def tile_at(d):
        return lax.rem(y + d, ny)

    barrier = pltpu.get_barrier_semaphore()
    peers = [(right, b), (left, b)]
    peers += [(tile_at(d) * nz + z, b) for d in range(1, ny)]
    peers += [(grid_id, receiver_of(jnp.int32(j))) for j in range(1, nb)]
    for peer in peers:
        pl.semaphore_signal(barrier, inc=1, device_id=peer, device_id_type=MESH)

    quarter = lax.div(lax.broadcasted_iota(jnp.int32, (CG, 128), 1), CG)
    lane8 = lax.broadcasted_iota(jnp.int32, (8, 128), 1)
    for oh in range(8):
        flat = w_ref[:, oh * 4 * ROW : (oh + 1) * 4 * ROW].astype(F32)
        for ol in range(4):
            for t in range(3):
                at = (2 * ol + t) * 128
                piece = flat[:, at : at + 128]
                if ol:
                    piece = pltpu.roll(piece, 128 - CG * ol, 1)
                    if t < 2:
                        after = pltpu.roll(flat[:, at + 128 : at + 256], 128 - CG * ol, 1)
                        piece = jnp.where(lane8 < 128 - CG * ol, piece, after)
                flat_a[t, pl.ds(oh * 4 + ol, EXP, stride=CG), :] = piece
    for h in range(2):
        for t in range(3):
            flat_t[h, t * 128 : (t + 1) * 128, :] = flat_a[t, h * 128 : (h + 1) * 128, :].T

    def turned(value):
        return [value] + [pltpu.roll(value, CG * k, 1) for k in range(1, 4)]

    for h in range(2):
        for th in range(2):
            turns = [turned(flat_t[h, pl.ds(th * 4 + tl, CG, stride=TAPS), :]) for tl in range(4)]
            for el in range(4):
                unit = turns[0][-el % 4]
                for tl in range(1, 4):
                    unit = jnp.where(quarter == tl, turns[tl][(tl - el) % 4], unit)
                wl[4 * h + el, th * CG : (th + 1) * CG, :] = unit.astype(BF)
        turns = turned(flat_t[h, pl.ds(8, CG, stride=TAPS), :])
        for el in range(4):
            low, high = turns[-el % 4][:16], turns[(1 - el) % 4][16:]
            unit = jnp.where(quarter[:16] == 0, low, jnp.where(quarter[:16] == 1, high, 0.0))
            wl[4 * h + el, 64:80, :] = unit.astype(BF)

    gates = jax.nn.sigmoid(logit_ref[...])
    gate_rows[...] = jnp.broadcast_to(gates, (128, 128)).T
    pl.semaphore_wait(barrier, len(peers))

    def act_copy(which, j):
        src, dst = ((dy_hbm, dyg), (x_hbm, xg))[which]
        peer = receiver_of(j)
        return pltpu.make_async_remote_copy(
            src_ref=src.at[0, pl.ds(pl.multiple_of(peer * CG, CG), CG), :],
            dst_ref=dst.at[b],
            send_sem=act_send.at[which, j],
            recv_sem=act_recv.at[which, j],
            device_id=(grid_id, peer),
            device_id_type=MESH,
        )

    def act_local(which):
        src, dst = ((dy_hbm, dyg), (x_hbm, xg))[which]
        return pltpu.make_async_copy(
            src.at[0, pl.ds(pl.multiple_of(b * CG, CG), CG), :], dst.at[b], act_loc.at[which]
        )

    def ag_copy(way, s, c, first):
        origin = lax.rem(z + nz - (s - 1), nz) if way == 0 else lax.rem(z + (s - 1), nz)
        piece = pl.ds(c * ES, ES)
        return pltpu.make_async_remote_copy(
            src_ref=wl.at[piece] if first else wg.at[origin, piece],
            dst_ref=wg.at[origin, piece],
            send_sem=ag_send.at[way, s - 1, c],
            recv_sem=ag_recv.at[way, s - 1, c],
            device_id=(hop_to[way], b),
            device_id_type=MESH,
        )

    def wy_copy(d, rel):
        zo = lax.rem(z + rel, nz)
        return pltpu.make_async_remote_copy(
            src_ref=ws.at[d - 1, rel],
            dst_ref=wr.at[y, zo],
            send_sem=wy_send.at[d - 1, rel],
            recv_sem=wy_recv.at[d - 1, rel],
            device_id=(tile_at(d) * nz + z, b),
            device_id_type=MESH,
        )

    def gy_copy(d, rel):
        return pltpu.make_async_remote_copy(
            src_ref=gs.at[d - 1, rel],
            dst_ref=gr.at[d, rel],
            send_sem=gy_send.at[d - 1, rel],
            recv_sem=gy_recv.at[d - 1, rel],
            device_id=(tile_at(d) * nz + z, b),
            device_id_type=MESH,
        )

    def rs_copy(way, t, c):
        return pltpu.make_async_remote_copy(
            src_ref=rs.at[way, t, c],
            dst_ref=rr.at[way, t + 1, c],
            send_sem=rs_send.at[way, t, c],
            recv_sem=rs_recv.at[way, t, c],
            device_id=(hop_to[way], b),
            device_id_type=MESH,
        )

    def dx_copy(j):
        s = sender_of(j)
        return pltpu.make_async_remote_copy(
            src_ref=dxs.at[s],
            dst_ref=dx_hbm.at[0, pl.ds(pl.multiple_of(b * CG, CG), CG), :],
            send_sem=dx_send.at[j],
            recv_sem=dx_recv.at[j],
            device_id=(grid_id, s),
            device_id_type=MESH,
        )

    def dot_copy(j):
        return pltpu.make_async_remote_copy(
            src_ref=dots_s,
            dst_ref=dots_r.at[j],
            send_sem=dot_send.at[j],
            recv_sem=dot_recv.at[j],
            device_id=(grid_id, receiver_of(j)),
            device_id_type=MESH,
        )

    act_local(0).start()
    act_local(1).start()
    for j in range(1, nb):
        act_copy(0, jnp.int32(j)).start()
        act_copy(1, jnp.int32(j)).start()
    for way in (0, 1):
        for c in range(NSUB):
            if half > 1 or (c < NSUB // 2) == (way == 0):
                ag_copy(way, 1, c, True).start()

    lane = lax.broadcasted_iota(jnp.int32, (8, PIX), 1)
    column = lax.rem(lane, SIDE)
    row = lax.div(lane, SIDE)
    for t in range(TAPS):
        down, over = t // 3 - 1, t % 3 - 1
        inside = (row - down >= 0) & (row - down < SIDE) & (column - over >= 0) & (column - over < SIDE)
        tap_mask[t] = jnp.where(inside, 1.0, 0.0).astype(F32)
    tail_row = lax.div(lax.broadcasted_iota(jnp.int32, (CG, 128), 0), 16)
    tail_lane = lax.div(lax.broadcasted_iota(jnp.int32, (CG, 128), 1), CG)
    tail = jnp.where(tail_row == tail_lane, 1.0, 0.0).astype(F32)
    tail_mask[...] = tail
    tail_mask_bf[...] = tail.astype(BF)
    parts[...] = jnp.zeros_like(parts)
    for c in range(NSUB):
        for way in (0, 1):
            rr[way, 0, c] = jnp.zeros((ES, UR, 128), BF)
        rr[1 if c < NSUB // 2 else 0, 1, c] = jnp.zeros((ES, UR, 128), BF)

    def expert_of(tile, zo):
        return lax.rem(tab_ref[tile, y * nz + zo], EXP)

    def pick(rel):
        zo = lax.rem(z + rel, nz)
        block[...] = wg[zo]
        wr[y, zo] = block[expert_of(y, zo)]
        for d in range(1, ny):
            ws[d - 1, rel] = block[expert_of(tile_at(d), zo)]

    def send_picks(rel):
        for d in range(1, ny):
            wy_copy(d, rel).start()

    def route_at(s, p, k):
        return (p * TOP + k) * nb + s

    def patch_lanes(p):
        return pl.ds(pl.multiple_of(p * PIX, PIX), PIX)

    def grad_patch(j, p):
        s = sender_of(j)
        index = s * pcol + p
        dy = dyg[s, :, patch_lanes(p)].astype(F32).reshape(CG // 8, 8, PIX)
        for t in range(TAPS):
            shift = ((t // 3 - 1) * SIDE + (t % 3 - 1)) % PIX
            moved = dy if shift == 0 else pltpu.roll(dy, shift, 2) * tap_mask[t][None]
            moved = moved.reshape(CG, PIX).astype(BF)
            if t < TAPS - 1:
                taps_buf[index, t * CG : (t + 1) * CG, :] = moved
            else:
                for k in range(4):
                    taps_buf[index, (t + k) * CG : (t + k + 1) * CG, :] = moved
        xp = xg[s, :, patch_lanes(p)]
        dims = (((1,), (1,)), ((), ()))
        main = lax.dot_general(xp, taps_buf[index, : 8 * CG, :], dims, preferred_element_type=F32)
        last = lax.dot_general(xp, taps_buf[index, 8 * CG :, :], dims, preferred_element_type=F32)
        last = last * tail_mask[...]
        gb[index, 0:32, :] = main[:, :128]
        gb[index, 32:64, :] = main[:, 128:]
        gb[index, 64:80, :] = last[:16] + last[16:]

    def grad_stage(rel):
        zo = lax.rem(z + rel, nz)
        for d in range(ny):
            route = lax.div(tab_ref[y, tile_at(d) * nz + zo], EXP)
            patch = lax.rem(route, nb) * pcol + lax.div(route, TOP * nb)
            value = (gb[patch] * gate_rows[pl.ds(route, 1), :]).astype(BF)
            if d == 0:
                gr[0, rel] = value
            else:
                gs[d - 1, rel] = value

    def route_unit(route):
        owner = lax.div(rows_ref[y, route], EXP)
        return wr[lax.div(owner, nz), lax.rem(owner, nz)]

    def dx_patch(j, p):
        s = sender_of(j)
        index = s * pcol + p
        mains, tails = [], []
        for k in range(TOP):
            unit = route_unit(route_at(s, p, k))
            mains.append(jnp.concatenate([unit[0:32], unit[32:64]], axis=1))
            tails.append(jnp.concatenate([unit[64:80], unit[64:80]], axis=0) * tail_mask_bf[...])
        adjoint = jnp.dot(
            jnp.concatenate(mains, axis=0), taps_buf[index, : 8 * CG, :], preferred_element_type=F32
        ) + jnp.dot(
            jnp.concatenate(tails, axis=0), taps_buf[index, 8 * CG :, :], preferred_element_type=F32
        )
        xp = xg[s, :, patch_lanes(p)].astype(F32)
        total = jnp.zeros((CG, PIX), F32)
        for k in range(TOP):
            one = adjoint[k * CG : (k + 1) * CG]
            prod = xp * one
            prod = (prod[0:8] + prod[8:16]) + (prod[16:24] + prod[24:32])
            prod = prod[:, :128] + prod[:, 128:]
            parts[pl.ds(route_at(s, p, k), 1), :] = jnp.sum(prod, axis=0, keepdims=True)
            gate = gate_rows[pl.ds(route_at(s, p, k), 1), :]
            gate = jnp.concatenate([gate, gate], axis=1)
            total = total + (gate * one).astype(BF).astype(F32)
        dxs[s, :, patch_lanes(p)] = total.astype(BF)

    def own_part(rel, e):
        zo = lax.rem(z + rel, nz)
        total = None
        for d in range(ny):
            tile = lax.rem(y + ny - d, ny)
            hit = jnp.where(expert_of(tile, zo) == e, 1.0, 0.0).astype(F32)
            term = gr[d, rel].astype(F32) * hit
            total = term if total is None else total + term
        return total

    def rs_add(way, t, c):
        rel = half - t if way == 0 else nz - half + t
        for k in range(ES):
            value = own_part(rel, c * ES + k) + rr[way, t, c, k].astype(F32)
            rs[way, t, c, k] = value.astype(BF)

    def wait_grads(rel):
        for d in range(1, ny):
            gy_copy(d, rel).wait_recv()

    wg[z] = wl[...]
    pick(jnp.int32(0))

    def gather_tick(k):
        s = lax.div(k, NSUB) + 1
        c = lax.rem(k, NSUB)
        low = c < NSUB // 2

        @pl.when(k < ticks)
        def _():
            for way in (0, 1):
                mine = low if way == 0 else jnp.logical_not(low)

                @pl.when(jnp.logical_or(s < half, mine))
                def _():
                    ag_copy(way, s, c, False).wait_recv()

                @pl.when(jnp.logical_or(s + 1 < half, jnp.logical_and(s + 1 == half, mine)))
                def _():
                    ag_copy(way, s + 1, c, False).start()

        @pl.when(jnp.logical_and(k <= ticks, c == 0))
        def _():
            send_picks(s - 1)

            @pl.when(jnp.logical_and(s > 1, s <= half))
            def _():
                send_picks(nz - s + 1)

        @pl.when(jnp.logical_and(k < ticks, c == NSUB - 1))
        def _():
            pick(s)

            @pl.when(s < half)
            def _():
                pick(nz - s)

    def grad_tick(i):
        j = lax.div(i, pcol)

        @pl.when(lax.rem(i, pcol) == 0)
        def _():
            @pl.when(j == 0)
            def _():
                act_local(0).wait()
                act_local(1).wait()

            @pl.when(j > 0)
            def _():
                act_copy(0, j).wait_recv()
                act_copy(1, j).wait_recv()

        def one(n, carry):
            grad_patch(j, lax.rem(i, pcol) + n)
            return carry

        lax.fori_loop(0, PER_TICK, one, 0)

    def stage_tick(k):
        count = nz // stage_ticks

        def rel_of(n):
            i = k * count + n
            return lax.rem(half + lax.div(i + 1, 2) * (1 - 2 * lax.rem(i, 2)) + nz, nz)

        def stage(n, carry):
            grad_stage(rel_of(n))
            return carry

        def send(n, carry):
            for d in range(1, ny):
                gy_copy(d, rel_of(n)).start()
            return carry

        lax.fori_loop(0, count, stage, 0)
        lax.fori_loop(0, count, send, 0)

    def scatter_start(k):
        t = lax.div(k, NSUB)
        c = lax.rem(k, NSUB)
        low = c < NSUB // 2

        @pl.when(c == 0)
        def _():
            wait_grads(half - t)

            @pl.when(t > 0)
            def _():
                wait_grads(nz - half + t)

        for way in (0, 1):
            mine = low if way == 0 else jnp.logical_not(low)

            @pl.when(jnp.logical_or(t > 1, jnp.logical_and(t == 1, mine)))
            def _():
                rs_copy(way, t - 1, c).wait_recv()

            rs_add(way, t, c)

    def scatter_send(k):
        t = lax.div(k, NSUB)
        c = lax.rem(k, NSUB)
        low = c < NSUB // 2
        for way in (0, 1):
            mine = low if way == 0 else jnp.logical_not(low)

            @pl.when(jnp.logical_or(t > 0, mine))
            def _():
                rs_copy(way, t, c).start()

    def dx_spot(i):
        return nb - 1 - lax.div(i, pcol), lax.rem(i, pcol)

    def dx_flush(i):
        j, p = dx_spot(i - PER_TICK)

        @pl.when(jnp.logical_and(p == pcol - PER_TICK, j > 0))
        def _():
            dx_copy(j).start()

    def wait_kernels(rel, carry):
        for d in range(1, ny):
            wy_copy(d, rel).wait_recv()
        return carry

    def phase_grad(k, carry):
        gather_tick(k)

        @pl.when(k >= grad_from)
        def _():
            grad_tick((k - grad_from) * PER_TICK)

        return carry

    def phase_stage(k, carry):
        gather_tick(k)

        @pl.when(k < stage_from + stage_ticks)
        def _():
            stage_tick(k - stage_from)

        return carry

    def phase_both(k, carry):
        gather_tick(k)
        scatter_start(k - rs_from)
        scatter_send(k - rs_from)
        return carry

    def phase_dx(k, carry):
        scatter_start(k - rs_from)
        first = (k - dx_from) * PER_TICK

        def one(n, carry):
            j, p = dx_spot(first)
            dx_patch(j, p + n)
            return carry

        @pl.when(first < patches)
        def _():
            one(0, 0)

        scatter_send(k - rs_from)

        @pl.when(jnp.logical_and(first > 0, first <= patches))
        def _():
            dx_flush(first)

        @pl.when(first < patches)
        def _():
            lax.fori_loop(1, PER_TICK, one, 0)

        return carry

    lax.fori_loop(0, stage_from, phase_grad, 0)
    lax.fori_loop(stage_from, rs_from, phase_stage, 0)
    lax.fori_loop(rs_from, dx_from, phase_both, 0)
    lax.fori_loop(0, nz, wait_kernels, 0)
    lax.fori_loop(dx_from, all_ticks, phase_dx, 0)

    own_dx = pltpu.make_async_copy(
        dxs.at[b], dx_hbm.at[0, pl.ds(pl.multiple_of(b * CG, CG), CG), :], out_sem.at[0]
    )
    own_dx.start()
    dots = jnp.sum(parts[...].T, axis=0, keepdims=True).astype(BF).astype(F32)
    dots_s[...] = jnp.broadcast_to(dots, (8, 128))

    wait_grads(jnp.int32(0))
    last = half - 1
    for c in range(NSUB):
        for way in (0, 1):
            if half > 1 or (c < NSUB // 2) == (way == 0):
                rs_copy(way, last, c).wait_recv()
        if c == 0:
            for j in range(1, nb):
                dot_copy(jnp.int32(j)).start()
        for k in range(ES):
            value = own_part(jnp.int32(0), c * ES + k)
            dw_v[c * ES + k] = value + rr[0, half, c, k].astype(F32) + rr[1, half, c, k].astype(F32)
    for h in range(2):
        for th in range(2):
            turns = [turned(dw_v[4 * h + el, th * CG : (th + 1) * CG, :]) for el in range(4)]
            for tl in range(4):
                value = turns[0][-tl % 4]
                for el in range(1, 4):
                    value = jnp.where(quarter == el, turns[el][(el - tl) % 4], value)
                flat_t[h, pl.ds(th * 4 + tl, CG, stride=TAPS), :] = value
        value = None
        for el in range(4):
            turns = turned(dw_v[4 * h + el, 64:80, :])
            both = jnp.concatenate([turns[el], turns[(el - 1) % 4]], axis=0)
            value = both if value is None else jnp.where(quarter == el, both, value)
        flat_t[h, pl.ds(8, CG, stride=TAPS), :] = value
    for h in range(2):
        for t in range(3):
            flat_a[t, h * 128 : (h + 1) * 128, :] = flat_t[h, t * 128 : (t + 1) * 128, :].T
    lane64 = lax.broadcasted_iota(jnp.int32, (8 * EXP, 128), 1)
    tiles = [None] * TAPS
    for ol in range(4):
        for t in range(3):
            piece = flat_a[t, pl.ds(ol, 8 * EXP, stride=4), :]
            if ol:
                piece = pltpu.roll(piece, CG * ol, 1)
            at = 2 * ol + t
            if t == 2:
                keep = (lane64 >= CG * ol) & (lane64 < CG * (ol + 1))
            else:
                keep = lane64 >= CG * ol
            tiles[at] = jnp.where(keep, piece, 0.0 if tiles[at] is None else tiles[at])
            if ol and t < 2:
                at += 1
                tiles[at] = jnp.where(lane64 < CG * ol, piece, 0.0 if tiles[at] is None else tiles[at])
    for q in range(TAPS):
        out_v[pl.ds(q, 8 * EXP, stride=TAPS), :] = tiles[q]
    out_dw = pltpu.make_async_copy(out_v, dw_hbm, out_sem.at[1])
    out_dw.start()

    total = dots_s[...]
    for j in range(1, nb):
        dot_copy(jnp.int32(j)).wait_recv()
        total = total + dots_r[j]
    total = gates * (1.0 - gates) * total[:1] * (1.0 / SIDE)
    for p in range(pcol):
        for k in range(TOP):
            spot = (p * TOP + k) * nb
            turn = total if spot == 0 else pltpu.roll(total, 128 - spot, 1)
            gg_ref[p, k : k + 1, :] = turn[:, :nb]

    for j in range(1, nb):
        act_copy(0, jnp.int32(j)).wait_send()
        act_copy(1, jnp.int32(j)).wait_send()
        dot_copy(jnp.int32(j)).wait_send()
        dx_copy(jnp.int32(j)).wait_send()
        dx_copy(jnp.int32(j)).wait_recv()

    def drain_ring(k, carry):
        s = lax.div(k, NSUB)
        c = lax.rem(k, NSUB)
        low = c < NSUB // 2
        for way in (0, 1):
            mine = low if way == 0 else jnp.logical_not(low)

            @pl.when(jnp.logical_or(s + 1 < half, mine))
            def _():
                ag_copy(way, s + 1, c, False).wait_send()

            @pl.when(jnp.logical_or(s > 0, mine))
            def _():
                rs_copy(way, s, c).wait_send()

        return carry

    lax.fori_loop(0, ticks, drain_ring, 0)

    def drain_rows(rel, carry):
        for d in range(1, ny):
            wy_copy(d, rel).wait_send()
            gy_copy(d, rel).wait_send()
        return carry

    lax.fori_loop(0, nz, drain_rows, 0)
    own_dx.wait()
    out_dw.wait()


def per_device(nz, inputs, cotangent, weights, gate_logits, routes):
    grid_size = lax.axis_size("grid")
    nb = lax.axis_size("batch")
    ny = grid_size // nz
    half = nz // 2
    _, channels, width = inputs.shape
    pcol = width // PIX
    patches = nb * pcol
    count = patches * TOP
    index = lax.axis_index("grid")
    y, z = index // nz, index % nz

    near = routes.reshape(nb, ny, nz, pcol, TOP)
    near = lax.dynamic_index_in_dim(near, z, 2, keepdims=False)
    rows = near.transpose(1, 2, 3, 0).reshape(ny, count)
    code = jnp.arange(count, dtype=jnp.int32)[None, :] * EXP + rows % EXP
    named = (rows // EXP)[:, None, :] == jnp.arange(grid_size, dtype=jnp.int32)[None, :, None]
    table = jnp.sum(jnp.where(named, code[:, None, :], 0), axis=2)
    own = lax.dynamic_slice_in_dim(gate_logits, index * pcol, pcol, 1).transpose(1, 2, 0).reshape(1, count)
    logits = jnp.pad(own, ((0, 0), (0, 128 - count)))

    vmem, smem, hbm = (
        pl.BlockSpec(memory_space=pltpu.VMEM),
        pl.BlockSpec(memory_space=pltpu.SMEM),
        pl.BlockSpec(memory_space=pl.ANY),
    )
    dma = pltpu.SemaphoreType.DMA
    d_inputs, d_flat, grads = pl.pallas_call(
        functools.partial(step_kernel, ny, nz, nb, pcol),
        out_shape=(
            jax.ShapeDtypeStruct(inputs.shape, BF),
            jax.ShapeDtypeStruct((EXP * ROW // 4, 128), F32),
            jax.ShapeDtypeStruct((pcol, TOP, nb), F32),
        ),
        in_specs=[hbm, hbm, vmem, smem, smem, vmem],
        out_specs=(hbm, hbm, vmem),
        scratch_shapes=[
            pltpu.VMEM((nb, CG, width), BF),
            pltpu.VMEM((nb, CG, width), BF),
            pltpu.VMEM((patches, 12 * CG, PIX), BF),
            pltpu.VMEM((nz, EXP, UR, 128), BF),
            pltpu.VMEM((ny - 1, nz, UR, 128), BF),
            pltpu.VMEM((ny, nz, UR, 128), BF),
            pltpu.VMEM((patches, UR, 128), F32),
            pltpu.VMEM((ny - 1, nz, UR, 128), BF),
            pltpu.VMEM((ny, nz, UR, 128), BF),
            pltpu.VMEM((2, half + 1, NSUB, ES, UR, 128), BF),
            pltpu.VMEM((2, half, NSUB, ES, UR, 128), BF),
            pltpu.VMEM((nb, CG, width), BF),
            pltpu.VMEM((128, 128), F32),
            pltpu.VMEM((8, 128), F32),
            pltpu.VMEM((nb, 8, 128), F32),
            pltpu.VMEM((EXP, UR, 128), F32),
            pltpu.VMEM((TAPS, 8, PIX), F32),
            pltpu.VMEM((CG, 128), F32),
            pltpu.VMEM((CG, 128), BF),
            pltpu.VMEM((EXP, UR, 128), BF),
            pltpu.VMEM((EXP, UR, 128), BF),
            pltpu.VMEM((3, EXP * CG, 128), F32),
            pltpu.VMEM((2, 3 * 128, 128), F32),
            pltpu.VMEM((EXP * ROW // 4, 128), F32),
            pltpu.VMEM((128, 128), F32),
            dma((2, nb)), dma((2, nb)), dma((2,)),
            dma((2, half, NSUB)), dma((2, half, NSUB)),
            dma((ny - 1, nz)), dma((ny - 1, nz)),
            dma((ny - 1, nz)), dma((ny - 1, nz)),
            dma((2, half, NSUB)), dma((2, half, NSUB)),
            dma((nb,)), dma((nb,)), dma((nb,)), dma((nb,)), dma((2,)),
        ],
        compiler_params=pltpu.CompilerParams(collective_id=0, has_side_effects=True),
        name="expert_step",
    )(inputs, cotangent, weights.reshape(EXP, CG * ROW), table, rows, logits)

    d_weights = (d_flat * (1.0 / SIDE)).reshape(weights.shape)
    gate_grad = grads.transpose(2, 0, 1)
    return (d_inputs, d_weights, gate_grad)


def solution(mesh):
    grid_size = mesh.shape["grid"]
    nz = Z_SIZE if grid_size % Z_SIZE == 0 else grid_size // 2
    placed = (
        P("batch", None, "grid"),
        P("batch", None, "grid"),
        P("grid", "batch", None),
        P(),
        P(),
    )
    return jax.shard_map(
        functools.partial(per_device, nz),
        mesh=mesh,
        in_specs=placed,
        out_specs=(P("batch", None, "grid"), P("grid", "batch", None), P(None, "grid", None)),
        check_vma=False,
    )
```

```python
import functools

import jax
import jax.numpy as jnp
from jax import lax
from jax.experimental import pallas as pl
from jax.experimental.pallas import tpu as pltpu
from jax.sharding import PartitionSpec as P

MESH = pl.DeviceIdType.MESH
CG = 32
SIDE = 16
PIX = SIDE * SIDE
TAPS = 9
ROW = CG * TAPS
EXP = 8
TOP = 2
NSUB = 4
ES = EXP // NSUB
DX_GAP = 4
UR = 80
MR = 64
PR = ES * MR + 16
BF = jnp.bfloat16
F32 = jnp.float32
Z_SIZE = 16


def step_kernel(
    ny, nz, nb, pcol,
    x_hbm, dy_hbm, w_ref, tab_ref, rows_ref, logit_ref,
    dx_hbm, dw_hbm, gg_ref,
    xg, dyg, taps_buf, wg, ws, wr, gb, gs, gr, rr, rs, dxs, parts, dots_s, dots_r, dw_v,
    tap_mask, tail_mask, tail_mask_bf, block, wl, flat_a, flat_t, out_v, gate_rows,
    act_send, act_recv, act_loc, ag_send, ag_recv, wy_send, wy_recv, gy_send, gy_recv,
    rs_send, rs_recv, dx_send, dx_recv, dot_send, dot_recv, out_sem,
):
    half = nz // 2
    nx = nb // 2
    patches = nb * pcol
    ticks = half * NSUB
    stage_from = nb
    stage_ticks = 4 if nz >= 16 else 2
    rs_from = stage_from + stage_ticks + 1
    pick_from = ticks - 2 * half
    dx_from = ticks + DX_GAP
    rs_end = rs_from + ticks
    all_ticks = max(rs_end, dx_from + nb)
    grid_id = lax.axis_index("grid")
    b = lax.axis_index("batch")
    y = lax.div(grid_id, nz)
    z = lax.rem(grid_id, nz)
    xi = lax.div(b, 2)
    core = lax.rem(b, 2)
    right = y * nz + lax.rem(z + 1, nz)
    left = y * nz + lax.rem(z + nz - 1, nz)
    hop_to = (right, left)

    def split(j):
        q = lax.div(j, 2)
        far = q + lax.div(q, 2) * (1 - 2 * lax.rem(q, 2))
        return far, lax.rem(j, 2)

    def sender_of(j):
        far, other = split(j)
        return lax.rem(xi + nx - far, nx) * 2 + lax.rem(core + other, 2)

    def receiver_of(j):
        far, other = split(j)
        return lax.rem(xi + far, nx) * 2 + lax.rem(core + other, 2)

    def tile_at(d):
        return lax.rem(y + d, ny)

    barrier = pltpu.get_barrier_semaphore()
    peers = [(right, b), (left, b)]
    peers += [(tile_at(d) * nz + z, b) for d in range(1, ny)]
    peers += [(grid_id, receiver_of(jnp.int32(j))) for j in range(1, nb)]
    for peer in peers:
        pl.semaphore_signal(barrier, inc=1, device_id=peer, device_id_type=MESH)

    quarter = lax.div(lax.broadcasted_iota(jnp.int32, (CG, 128), 1), CG)
    lane8 = lax.broadcasted_iota(jnp.int32, (8, 128), 1)
    for oh in range(8):
        flat = w_ref[:, oh * 4 * ROW : (oh + 1) * 4 * ROW].astype(F32)
        for ol in range(4):
            for t in range(3):
                at = (2 * ol + t) * 128
                piece = flat[:, at : at + 128]
                if ol:
                    piece = pltpu.roll(piece, 128 - CG * ol, 1)
                    if t < 2:
                        after = pltpu.roll(flat[:, at + 128 : at + 256], 128 - CG * ol, 1)
                        piece = jnp.where(lane8 < 128 - CG * ol, piece, after)
                flat_a[t, pl.ds(oh * 4 + ol, EXP, stride=CG), :] = piece
    for h in range(2):
        for t in range(3):
            flat_t[h, t * 128 : (t + 1) * 128, :] = flat_a[t, h * 128 : (h + 1) * 128, :].T

    def turned(value):
        return [value] + [pltpu.roll(value, CG * k, 1) for k in range(1, 4)]

    for h in range(2):
        for th in range(2):
            turns = [turned(flat_t[h, pl.ds(th * 4 + tl, CG, stride=TAPS), :]) for tl in range(4)]
            for el in range(4):
                unit = turns[0][-el % 4]
                for tl in range(1, 4):
                    unit = jnp.where(quarter == tl, turns[tl][(tl - el) % 4], unit)
                at = el % 2 * MR + th * CG
                wl[2 * h + el // 2, at : at + CG, :] = unit.astype(BF)
        turns = turned(flat_t[h, pl.ds(8, CG, stride=TAPS), :])
        for pair in range(2):
            unit = jnp.zeros((16, 128), F32)
            for spot in range(4):
                el, ih = 2 * pair + spot // 2, spot % 2
                unit = jnp.where(quarter[:16] == spot, turns[(spot - el) % 4][16 * ih : 16 * ih + 16], unit)
            wl[2 * h + pair, ES * MR :, :] = unit.astype(BF)

    gates = jax.nn.sigmoid(logit_ref[...])
    gate_rows[...] = jnp.broadcast_to(gates, (128, 128)).T
    pl.semaphore_wait(barrier, len(peers))

    def act_copy(which, j):
        src, dst = ((dy_hbm, dyg), (x_hbm, xg))[which]
        peer = receiver_of(j)
        return pltpu.make_async_remote_copy(
            src_ref=src.at[0, pl.ds(pl.multiple_of(peer * CG, CG), CG), :],
            dst_ref=dst.at[b],
            send_sem=act_send.at[which, j],
            recv_sem=act_recv.at[which, j],
            device_id=(grid_id, peer),
            device_id_type=MESH,
        )

    def act_local(which):
        src, dst = ((dy_hbm, dyg), (x_hbm, xg))[which]
        return pltpu.make_async_copy(
            src.at[0, pl.ds(pl.multiple_of(b * CG, CG), CG), :], dst.at[b], act_loc.at[which]
        )

    def ag_copy(way, s, c, first):
        origin = lax.rem(z + nz - (s - 1), nz) if way == 0 else lax.rem(z + (s - 1), nz)
        return pltpu.make_async_remote_copy(
            src_ref=wl.at[c] if first else wg.at[origin, c],
            dst_ref=wg.at[origin, c],
            send_sem=ag_send.at[way, s - 1, c],
            recv_sem=ag_recv.at[way, s - 1, c],
            device_id=(hop_to[way], b),
            device_id_type=MESH,
        )

    def wy_copy(d, rel):
        zo = lax.rem(z + rel, nz)
        return pltpu.make_async_remote_copy(
            src_ref=ws.at[d - 1, rel],
            dst_ref=wr.at[y, zo],
            send_sem=wy_send.at[d - 1, rel],
            recv_sem=wy_recv.at[d - 1, rel],
            device_id=(tile_at(d) * nz + z, b),
            device_id_type=MESH,
        )

    def gy_copy(d, rel):
        return pltpu.make_async_remote_copy(
            src_ref=gs.at[d - 1, rel],
            dst_ref=gr.at[d, rel],
            send_sem=gy_send.at[d - 1, rel],
            recv_sem=gy_recv.at[d - 1, rel],
            device_id=(tile_at(d) * nz + z, b),
            device_id_type=MESH,
        )

    def rs_copy(way, t, c):
        return pltpu.make_async_remote_copy(
            src_ref=rs.at[way, t, c],
            dst_ref=rr.at[way, t + 1, c],
            send_sem=rs_send.at[way, t, c],
            recv_sem=rs_recv.at[way, t, c],
            device_id=(hop_to[way], b),
            device_id_type=MESH,
        )

    def dx_copy(j):
        s = sender_of(j)
        return pltpu.make_async_remote_copy(
            src_ref=dxs.at[s],
            dst_ref=dx_hbm.at[0, pl.ds(pl.multiple_of(b * CG, CG), CG), :],
            send_sem=dx_send.at[j],
            recv_sem=dx_recv.at[j],
            device_id=(grid_id, s),
            device_id_type=MESH,
        )

    def dot_copy(j):
        return pltpu.make_async_remote_copy(
            src_ref=dots_s,
            dst_ref=dots_r.at[j],
            send_sem=dot_send.at[j],
            recv_sem=dot_recv.at[j],
            device_id=(grid_id, receiver_of(j)),
            device_id_type=MESH,
        )

    act_local(0).start()
    act_local(1).start()
    for j in range(1, nb):
        act_copy(0, jnp.int32(j)).start()
        act_copy(1, jnp.int32(j)).start()
    for way in (0, 1):
        for c in range(NSUB):
            if half > 1 or (c < NSUB // 2) == (way == 0):
                ag_copy(way, 1, c, True).start()

    lane = lax.broadcasted_iota(jnp.int32, (8, PIX), 1)
    column = lax.rem(lane, SIDE)
    row = lax.div(lane, SIDE)
    for t in range(TAPS):
        down, over = t // 3 - 1, t % 3 - 1
        inside = (row - down >= 0) & (row - down < SIDE) & (column - over >= 0) & (column - over < SIDE)
        tap_mask[t] = jnp.where(inside, 1.0, 0.0).astype(F32)
    tail_row = lax.div(lax.broadcasted_iota(jnp.int32, (CG, 128), 0), 16)
    tail_lane = lax.div(lax.broadcasted_iota(jnp.int32, (CG, 128), 1), CG)
    tail_mask[...] = jnp.where(lax.rem(tail_lane, 2) == tail_row, 1.0, 0.0).astype(F32)
    for k in range(2):
        tail_mask_bf[k] = jnp.where(tail_lane == 2 * k + tail_row, 1.0, 0.0).astype(F32).astype(BF)
    first_half = lax.broadcasted_iota(jnp.int32, (16, 128), 1) < 64
    parts[...] = jnp.zeros_like(parts)
    for c in range(NSUB):
        for way in (0, 1):
            rr[way, 0, c] = jnp.zeros((PR, 128), BF)
        rr[1 if c < NSUB // 2 else 0, 1, c] = jnp.zeros((PR, 128), BF)

    def expert_of(tile, zo):
        return lax.rem(tab_ref[tile, y * nz + zo], EXP)

    def pick(rel):
        zo = lax.rem(z + rel, nz)
        for e in range(EXP):
            at = e % 2 * MR
            block[e, :MR] = wg[zo, e // 2, at : at + MR, :]
            block[e, MR:] = wg[zo, e // 2, ES * MR :, :]
        wr[y, zo] = block[expert_of(y, zo)]
        for d in range(1, ny):
            ws[d - 1, rel] = block[expert_of(tile_at(d), zo)]

    def send_picks(rel):
        for d in range(1, ny):
            wy_copy(d, rel).start()

    def route_at(s, p, k):
        return (p * TOP + k) * nb + s

    def patch_lanes(p):
        return pl.ds(pl.multiple_of(p * PIX, PIX), PIX)

    def grad_patch(j, p):
        s = sender_of(j)
        index = s * pcol + p
        dy = dyg[s, :, patch_lanes(p)].astype(F32).reshape(CG // 8, 8, PIX)
        for t in range(TAPS):
            shift = ((t // 3 - 1) * SIDE + (t % 3 - 1)) % PIX
            moved = dy if shift == 0 else pltpu.roll(dy, shift, 2) * tap_mask[t][None]
            moved = moved.reshape(CG, PIX).astype(BF)
            if t < TAPS - 1:
                taps_buf[index, t * CG : (t + 1) * CG, :] = moved
            else:
                for k in range(4):
                    taps_buf[index, (t + k) * CG : (t + k + 1) * CG, :] = moved
        xp = xg[s, :, patch_lanes(p)]
        dims = (((1,), (1,)), ((), ()))
        main = lax.dot_general(xp, taps_buf[index, : 8 * CG, :], dims, preferred_element_type=F32)
        last = lax.dot_general(xp, taps_buf[index, 8 * CG :, :], dims, preferred_element_type=F32)
        last = last * tail_mask[...]
        gb[index, 0:32, :] = main[:, :128]
        gb[index, 32:64, :] = main[:, 128:]
        gb[index, 64:80, :] = last[:16] + last[16:]

    def grad_stage(rel):
        zo = lax.rem(z + rel, nz)
        for d in range(ny):
            route = lax.div(tab_ref[y, tile_at(d) * nz + zo], EXP)
            patch = lax.rem(route, nb) * pcol + lax.div(route, TOP * nb)
            value = (gb[patch] * gate_rows[pl.ds(route, 1), :]).astype(BF)
            if d == 0:
                gr[0, rel] = value
            else:
                gs[d - 1, rel] = value

    def route_unit(route):
        expert = rows_ref[y, route]
        owner = lax.div(expert, EXP)
        return wr[lax.div(owner, nz), lax.rem(owner, nz)], tail_mask_bf[lax.rem(expert, 2)]

    def dx_patch(j, p):
        s = sender_of(j)
        index = s * pcol + p
        mains, tails = [], []
        for k in range(TOP):
            unit, mask = route_unit(route_at(s, p, k))
            mains.append(jnp.concatenate([unit[0:32], unit[32:64]], axis=1))
            tails.append(jnp.concatenate([unit[64:80], unit[64:80]], axis=0) * mask)
        adjoint = jnp.dot(
            jnp.concatenate(mains, axis=0), taps_buf[index, : 8 * CG, :], preferred_element_type=F32
        ) + jnp.dot(
            jnp.concatenate(tails, axis=0), taps_buf[index, 8 * CG :, :], preferred_element_type=F32
        )
        xp = xg[s, :, patch_lanes(p)].astype(F32)
        total = jnp.zeros((CG, PIX), F32)
        for k in range(TOP):
            one = adjoint[k * CG : (k + 1) * CG]
            prod = xp * one
            prod = (prod[0:8] + prod[8:16]) + (prod[16:24] + prod[24:32])
            prod = prod[:, :128] + prod[:, 128:]
            parts[pl.ds(route_at(s, p, k), 1), :] = jnp.sum(prod, axis=0, keepdims=True)
            gate = gate_rows[pl.ds(route_at(s, p, k), 1), :]
            gate = jnp.concatenate([gate, gate], axis=1)
            total = total + (gate * one).astype(BF).astype(F32)
        dxs[s, :, patch_lanes(p)] = total.astype(BF)

    def own_piece(rel, c):
        zo = lax.rem(z + rel, nz)
        parts_of = [None] * 3
        for d in range(ny):
            expert = expert_of(lax.rem(y + ny - d, ny), zo)
            hits = [jnp.where(expert == c * ES + k, 1.0, 0.0).astype(F32) for k in range(ES)]
            main = gr[d, rel, :MR].astype(F32)
            last = gr[d, rel, MR:].astype(F32)
            terms = [main * hits[0], main * hits[1], last * jnp.where(first_half, hits[0], hits[1])]
            parts_of = [b if a is None else a + b for a, b in zip(parts_of, terms)]
        return parts_of

    piece_rows = (slice(0, MR), slice(MR, ES * MR), slice(ES * MR, PR))

    def rs_add(way, t, c):
        rel = half - t if way == 0 else nz - half + t
        for rows, value in zip(piece_rows, own_piece(rel, c)):
            rs[way, t, c, rows, :] = (value + rr[way, t, c, rows, :].astype(F32)).astype(BF)

    def wait_grads(rel):
        for d in range(1, ny):
            gy_copy(d, rel).wait_recv()

    wg[z] = wl[...]
    pick(jnp.int32(0))

    def gather_tick(k):
        s = lax.div(k, NSUB) + 1
        c = lax.rem(k, NSUB)
        low = c < NSUB // 2

        @pl.when(k < ticks)
        def _():
            for way in (0, 1):
                mine = low if way == 0 else jnp.logical_not(low)

                @pl.when(jnp.logical_or(s < half, mine))
                def _():
                    ag_copy(way, s, c, False).wait_recv()

                @pl.when(jnp.logical_or(s + 1 < half, jnp.logical_and(s + 1 == half, mine)))
                def _():
                    ag_copy(way, s + 1, c, False).start()

        turn = k - pick_from
        i = lax.div(turn, 2)

        @pl.when(jnp.logical_and(turn >= 0, jnp.logical_and(i * 2 == turn, i <= half)))
        def _():
            send_picks(i)

            @pl.when(jnp.logical_and(i > 0, i < half))
            def _():
                send_picks(nz - i)

        @pl.when(jnp.logical_and(k < ticks, c == NSUB - 1))
        def _():
            pick(s)

            @pl.when(s < half)
            def _():
                pick(nz - s)

    def grad_tick(j):
        @pl.when(j == 0)
        def _():
            act_local(0).wait()
            act_local(1).wait()

        @pl.when(j > 0)
        def _():
            act_copy(0, j).wait_recv()
            act_copy(1, j).wait_recv()

        def one(p, carry):
            grad_patch(j, p)
            return carry

        lax.fori_loop(0, pcol, one, 0)

    def stage_tick(k):
        count = nz // stage_ticks

        def rel_of(n):
            i = k * count + n
            return lax.rem(half + lax.div(i + 1, 2) * (1 - 2 * lax.rem(i, 2)) + nz, nz)

        def stage(n, carry):
            grad_stage(rel_of(n))
            return carry

        def send(n, carry):
            for d in range(1, ny):
                gy_copy(d, rel_of(n)).start()
            return carry

        lax.fori_loop(0, count, stage, 0)
        lax.fori_loop(0, count, send, 0)

    def scatter_start(k):
        t = lax.div(k, NSUB)
        c = lax.rem(k, NSUB)
        low = c < NSUB // 2

        @pl.when(c == 0)
        def _():
            wait_grads(half - t)

            @pl.when(t > 0)
            def _():
                wait_grads(nz - half + t)

        for way in (0, 1):
            mine = low if way == 0 else jnp.logical_not(low)

            @pl.when(jnp.logical_or(t > 1, jnp.logical_and(t == 1, mine)))
            def _():
                rs_copy(way, t - 1, c).wait_recv()

            rs_add(way, t, c)

    def scatter_send(k):
        t = lax.div(k, NSUB)
        c = lax.rem(k, NSUB)
        low = c < NSUB // 2
        for way in (0, 1):
            mine = low if way == 0 else jnp.logical_not(low)

            @pl.when(jnp.logical_or(t > 0, mine))
            def _():
                rs_copy(way, t, c).start()

    def wait_kernels(rel, carry):
        for d in range(1, ny):
            wy_copy(d, rel).wait_recv()
        return carry

    def phase_grad(k, carry):
        grad_tick(k)
        gather_tick(k)
        return carry

    def phase_stage(k, carry):
        gather_tick(k)

        @pl.when(k < stage_from + stage_ticks)
        def _():
            stage_tick(k - stage_from)

        return carry

    def phase_both(k, carry):
        gather_tick(k)
        scatter_start(k - rs_from)
        scatter_send(k - rs_from)
        return carry

    def phase_dx(k, carry):
        @pl.when(k < rs_end)
        def _():
            scatter_start(k - rs_from)

        j = nb - 1 - (k - dx_from)

        def one(p, carry):
            dx_patch(j, p)
            return carry

        @pl.when(j >= 0)
        def _():
            one(0, 0)

        @pl.when(k < rs_end)
        def _():
            scatter_send(k - rs_from)

        @pl.when(jnp.logical_and(j + 1 > 0, j + 1 < nb))
        def _():
            dx_copy(j + 1).start()

        @pl.when(j >= 0)
        def _():
            lax.fori_loop(1, pcol, one, 0)

        return carry

    lax.fori_loop(0, stage_from, phase_grad, 0)
    lax.fori_loop(stage_from, rs_from, phase_stage, 0)
    lax.fori_loop(rs_from, dx_from, phase_both, 0)
    lax.fori_loop(0, nz, wait_kernels, 0)
    lax.fori_loop(dx_from, all_ticks, phase_dx, 0)
    own_dx = pltpu.make_async_copy(
        dxs.at[b], dx_hbm.at[0, pl.ds(pl.multiple_of(b * CG, CG), CG), :], out_sem.at[0]
    )
    own_dx.start()
    dots = jnp.sum(parts[...].T, axis=0, keepdims=True).astype(BF).astype(F32)
    dots_s[...] = jnp.broadcast_to(dots, (8, 128))

    wait_grads(jnp.int32(0))
    last = half - 1
    for c in range(NSUB):
        for way in (0, 1):
            if half > 1 or (c < NSUB // 2) == (way == 0):
                rs_copy(way, last, c).wait_recv()
        if c == 0:
            for j in range(1, nb):
                dot_copy(jnp.int32(j)).start()
        value = [
            v + rr[0, half, c, rows, :].astype(F32) + rr[1, half, c, rows, :].astype(F32)
            for rows, v in zip(piece_rows, own_piece(jnp.int32(0), c))
        ]
        dw_v[ES * c, :MR] = value[0]
        dw_v[ES * c + 1, :MR] = value[1]
        dw_v[ES * c, MR:] = value[2]
        dw_v[ES * c + 1, MR:] = pltpu.roll(value[2], 64, 1)
    for h in range(2):
        for th in range(2):
            turns = [turned(dw_v[4 * h + el, th * CG : (th + 1) * CG, :]) for el in range(4)]
            for tl in range(4):
                value = turns[0][-tl % 4]
                for el in range(1, 4):
                    value = jnp.where(quarter == el, turns[el][(el - tl) % 4], value)
                flat_t[h, pl.ds(th * 4 + tl, CG, stride=TAPS), :] = value
        value = None
        for el in range(4):
            turns = turned(dw_v[4 * h + el, 64:80, :])
            both = jnp.concatenate([turns[el], turns[(el - 1) % 4]], axis=0)
            value = both if value is None else jnp.where(quarter == el, both, value)
        flat_t[h, pl.ds(8, CG, stride=TAPS), :] = value
    for h in range(2):
        for t in range(3):
            flat_a[t, h * 128 : (h + 1) * 128, :] = flat_t[h, t * 128 : (t + 1) * 128, :].T
    lane64 = lax.broadcasted_iota(jnp.int32, (8 * EXP, 128), 1)
    tiles = [None] * TAPS
    for ol in range(4):
        for t in range(3):
            piece = flat_a[t, pl.ds(ol, 8 * EXP, stride=4), :]
            if ol:
                piece = pltpu.roll(piece, CG * ol, 1)
            at = 2 * ol + t
            if t == 2:
                keep = (lane64 >= CG * ol) & (lane64 < CG * (ol + 1))
            else:
                keep = lane64 >= CG * ol
            tiles[at] = jnp.where(keep, piece, 0.0 if tiles[at] is None else tiles[at])
            if ol and t < 2:
                at += 1
                tiles[at] = jnp.where(lane64 < CG * ol, piece, 0.0 if tiles[at] is None else tiles[at])
    for q in range(TAPS):
        out_v[pl.ds(q, 8 * EXP, stride=TAPS), :] = tiles[q]
    out_dw = pltpu.make_async_copy(out_v, dw_hbm, out_sem.at[1])
    out_dw.start()

    total = dots_s[...]
    for j in range(1, nb):
        dot_copy(jnp.int32(j)).wait_recv()
        total = total + dots_r[j]
    total = gates * (1.0 - gates) * total[:1] * (1.0 / SIDE)
    for p in range(pcol):
        for k in range(TOP):
            spot = (p * TOP + k) * nb
            turn = total if spot == 0 else pltpu.roll(total, 128 - spot, 1)
            gg_ref[p, k : k + 1, :] = turn[:, :nb]

    for j in range(1, nb):
        act_copy(0, jnp.int32(j)).wait_send()
        act_copy(1, jnp.int32(j)).wait_send()
        dot_copy(jnp.int32(j)).wait_send()
        dx_copy(jnp.int32(j)).wait_send()
        dx_copy(jnp.int32(j)).wait_recv()

    def drain_ring(k, carry):
        s = lax.div(k, NSUB)
        c = lax.rem(k, NSUB)
        low = c < NSUB // 2
        for way in (0, 1):
            mine = low if way == 0 else jnp.logical_not(low)

            @pl.when(jnp.logical_or(s + 1 < half, mine))
            def _():
                ag_copy(way, s + 1, c, False).wait_send()

            @pl.when(jnp.logical_or(s > 0, mine))
            def _():
                rs_copy(way, s, c).wait_send()

        return carry

    lax.fori_loop(0, ticks, drain_ring, 0)

    def drain_rows(rel, carry):
        for d in range(1, ny):
            wy_copy(d, rel).wait_send()
            gy_copy(d, rel).wait_send()
        return carry

    lax.fori_loop(0, nz, drain_rows, 0)
    own_dx.wait()
    out_dw.wait()


def per_device(nz, inputs, cotangent, weights, gate_logits, routes):
    grid_size = lax.axis_size("grid")
    nb = lax.axis_size("batch")
    ny = grid_size // nz
    half = nz // 2
    _, channels, width = inputs.shape
    pcol = width // PIX
    patches = nb * pcol
    count = patches * TOP
    index = lax.axis_index("grid")
    y, z = index // nz, index % nz

    near = routes.reshape(nb, ny, nz, pcol, TOP)
    near = lax.dynamic_index_in_dim(near, z, 2, keepdims=False)
    rows = near.transpose(1, 2, 3, 0).reshape(ny, count)
    code = jnp.arange(count, dtype=jnp.int32)[None, :] * EXP + rows % EXP
    named = (rows // EXP)[:, None, :] == jnp.arange(grid_size, dtype=jnp.int32)[None, :, None]
    table = jnp.sum(jnp.where(named, code[:, None, :], 0), axis=2)
    own = lax.dynamic_slice_in_dim(gate_logits, index * pcol, pcol, 1).transpose(1, 2, 0).reshape(1, count)
    logits = jnp.pad(own, ((0, 0), (0, 128 - count)))

    vmem, smem, hbm = (
        pl.BlockSpec(memory_space=pltpu.VMEM),
        pl.BlockSpec(memory_space=pltpu.SMEM),
        pl.BlockSpec(memory_space=pl.ANY),
    )
    dma = pltpu.SemaphoreType.DMA
    d_inputs, d_flat, grads = pl.pallas_call(
        functools.partial(step_kernel, ny, nz, nb, pcol),
        out_shape=(
            jax.ShapeDtypeStruct(inputs.shape, BF),
            jax.ShapeDtypeStruct((EXP * ROW // 4, 128), F32),
            jax.ShapeDtypeStruct((pcol, TOP, nb), F32),
        ),
        in_specs=[hbm, hbm, vmem, smem, smem, vmem],
        out_specs=(hbm, hbm, vmem),
        scratch_shapes=[
            pltpu.VMEM((nb, CG, width), BF),
            pltpu.VMEM((nb, CG, width), BF),
            pltpu.VMEM((patches, 12 * CG, PIX), BF),
            pltpu.VMEM((nz, NSUB, PR, 128), BF),
            pltpu.VMEM((ny - 1, nz, UR, 128), BF),
            pltpu.VMEM((ny, nz, UR, 128), BF),
            pltpu.VMEM((patches, UR, 128), F32),
            pltpu.VMEM((ny - 1, nz, UR, 128), BF),
            pltpu.VMEM((ny, nz, UR, 128), BF),
            pltpu.VMEM((2, half + 1, NSUB, PR, 128), BF),
            pltpu.VMEM((2, half, NSUB, PR, 128), BF),
            pltpu.VMEM((nb, CG, width), BF),
            pltpu.VMEM((128, 128), F32),
            pltpu.VMEM((8, 128), F32),
            pltpu.VMEM((nb, 8, 128), F32),
            pltpu.VMEM((EXP, UR, 128), F32),
            pltpu.VMEM((TAPS, 8, PIX), F32),
            pltpu.VMEM((CG, 128), F32),
            pltpu.VMEM((2, CG, 128), BF),
            pltpu.VMEM((EXP, UR, 128), BF),
            pltpu.VMEM((NSUB, PR, 128), BF),
            pltpu.VMEM((3, EXP * CG, 128), F32),
            pltpu.VMEM((2, 3 * 128, 128), F32),
            pltpu.VMEM((EXP * ROW // 4, 128), F32),
            pltpu.VMEM((128, 128), F32),
            dma((2, nb)), dma((2, nb)), dma((2,)),
            dma((2, half, NSUB)), dma((2, half, NSUB)),
            dma((ny - 1, nz)), dma((ny - 1, nz)),
            dma((ny - 1, nz)), dma((ny - 1, nz)),
            dma((2, half, NSUB)), dma((2, half, NSUB)),
            dma((nb,)), dma((nb,)), dma((nb,)), dma((nb,)), dma((2,)),
        ],
        compiler_params=pltpu.CompilerParams(collective_id=0, has_side_effects=True),
        name="expert_step",
    )(inputs, cotangent, weights.reshape(EXP, CG * ROW), table, rows, logits)

    d_weights = (d_flat * (1.0 / SIDE)).reshape(weights.shape)
    gate_grad = grads.transpose(2, 0, 1)
    return (d_inputs, d_weights, gate_grad)


def solution(mesh):
    grid_size = mesh.shape["grid"]
    nz = Z_SIZE if grid_size % Z_SIZE == 0 else grid_size // 2
    placed = (
        P("batch", None, "grid"),
        P("batch", None, "grid"),
        P("grid", "batch", None),
        P(),
        P(),
    )
    return jax.shard_map(
        functools.partial(per_device, nz),
        mesh=mesh,
        in_specs=placed,
        out_specs=(P("batch", None, "grid"), P("grid", "batch", None), P(None, "grid", None)),
        check_vma=False,
    )
```

```python
import functools

import jax
import jax.numpy as jnp
from jax import lax
from jax.experimental import pallas as pl
from jax.experimental.pallas import tpu as pltpu
from jax.sharding import PartitionSpec as P

MESH = pl.DeviceIdType.MESH
CG = 32
SIDE = 16
PIX = SIDE * SIDE
TAPS = 9
ROW = CG * TAPS
EXP = 8
TOP = 2
NSUB = 4
ES = EXP // NSUB
DX_GAP = 4
UR = 80
MR = 64
PR = ES * MR + 16
BF = jnp.bfloat16
F32 = jnp.float32
Z_SIZE = 16


def step_kernel(
    ny, nz, nb, pcol,
    x_hbm, dy_hbm, w_ref, tab_ref, rows_ref, logit_ref,
    dx_hbm, dw_hbm, gg_ref,
    xg, dyg, taps_buf, wg, ws, wr, gb, gs, gr, rr, rs, dxs, parts, dots_s, dots_r, dw_v,
    tap_mask, tail_mask, tail_mask_bf, block, wl, flat_a, flat_t, out_v, gate_rows,
    act_send, act_recv, act_loc, ag_send, ag_recv, wy_send, wy_recv, gy_send, gy_recv,
    rs_send, rs_recv, dx_send, dx_recv, dot_send, dot_recv, out_sem,
):
    half = nz // 2
    nx = nb // 2
    patches = nb * pcol
    ticks = half * NSUB
    stage_from = nb
    stage_ticks = 4 if nz >= 16 else 2
    rs_from = stage_from + stage_ticks + 1
    pick_from = ticks - 2 * half
    dx_from = ticks + DX_GAP
    rs_end = rs_from + ticks
    all_ticks = max(rs_end, dx_from + nb)
    grid_id = lax.axis_index("grid")
    b = lax.axis_index("batch")
    y = lax.div(grid_id, nz)
    z = lax.rem(grid_id, nz)
    xi = lax.div(b, 2)
    core = lax.rem(b, 2)
    right = y * nz + lax.rem(z + 1, nz)
    left = y * nz + lax.rem(z + nz - 1, nz)
    hop_to = (right, left)

    def split(j):
        q = lax.div(j, 2)
        far = q + lax.div(q, 2) * (1 - 2 * lax.rem(q, 2))
        return far, lax.rem(j, 2)

    def sender_of(j):
        far, other = split(j)
        return lax.rem(xi + nx - far, nx) * 2 + lax.rem(core + other, 2)

    def receiver_of(j):
        far, other = split(j)
        return lax.rem(xi + far, nx) * 2 + lax.rem(core + other, 2)

    def tile_at(d):
        return lax.rem(y + d, ny)

    barrier = pltpu.get_barrier_semaphore()
    peers = [(right, b), (left, b)]
    peers += [(tile_at(d) * nz + z, b) for d in range(1, ny)]
    peers += [(grid_id, receiver_of(jnp.int32(j))) for j in range(1, nb)]
    for peer in peers:
        pl.semaphore_signal(barrier, inc=1, device_id=peer, device_id_type=MESH)

    quarter = lax.div(lax.broadcasted_iota(jnp.int32, (CG, 128), 1), CG)
    lane8 = lax.broadcasted_iota(jnp.int32, (8, 128), 1)
    for oh in range(8):
        flat = w_ref[:, oh * 4 * ROW : (oh + 1) * 4 * ROW].astype(F32)
        for ol in range(4):
            for t in range(3):
                at = (2 * ol + t) * 128
                piece = flat[:, at : at + 128]
                if ol:
                    piece = pltpu.roll(piece, 128 - CG * ol, 1)
                    if t < 2:
                        after = pltpu.roll(flat[:, at + 128 : at + 256], 128 - CG * ol, 1)
                        piece = jnp.where(lane8 < 128 - CG * ol, piece, after)
                flat_a[t, pl.ds(oh * 4 + ol, EXP, stride=CG), :] = piece
    for h in range(2):
        for t in range(3):
            flat_t[h, t * 128 : (t + 1) * 128, :] = flat_a[t, h * 128 : (h + 1) * 128, :].T

    def turned(value):
        return [value] + [pltpu.roll(value, CG * k, 1) for k in range(1, 4)]

    for h in range(2):
        for th in range(2):
            turns = [turned(flat_t[h, pl.ds(th * 4 + tl, CG, stride=TAPS), :]) for tl in range(4)]
            for el in range(4):
                unit = turns[0][-el % 4]
                for tl in range(1, 4):
                    unit = jnp.where(quarter == tl, turns[tl][(tl - el) % 4], unit)
                at = el % 2 * MR + th * CG
                wl[2 * h + el // 2, at : at + CG, :] = unit.astype(BF)
        turns = turned(flat_t[h, pl.ds(8, CG, stride=TAPS), :])
        for pair in range(2):
            unit = jnp.zeros((16, 128), F32)
            for spot in range(4):
                el, ih = 2 * pair + spot // 2, spot % 2
                unit = jnp.where(quarter[:16] == spot, turns[(spot - el) % 4][16 * ih : 16 * ih + 16], unit)
            wl[2 * h + pair, ES * MR :, :] = unit.astype(BF)

    gates = jax.nn.sigmoid(logit_ref[...])
    gate_rows[...] = jnp.broadcast_to(gates, (128, 128)).T
    pl.semaphore_wait(barrier, len(peers))

    def act_copy(which, j):
        src, dst = ((dy_hbm, dyg), (x_hbm, xg))[which]
        peer = receiver_of(j)
        return pltpu.make_async_remote_copy(
            src_ref=src.at[0, pl.ds(pl.multiple_of(peer * CG, CG), CG), :],
            dst_ref=dst.at[b],
            send_sem=act_send.at[which, j],
            recv_sem=act_recv.at[which, j],
            device_id=(grid_id, peer),
            device_id_type=MESH,
        )

    def act_local(which):
        src, dst = ((dy_hbm, dyg), (x_hbm, xg))[which]
        return pltpu.make_async_copy(
            src.at[0, pl.ds(pl.multiple_of(b * CG, CG), CG), :], dst.at[b], act_loc.at[which]
        )

    def ag_copy(way, s, c, first):
        origin = lax.rem(z + nz - (s - 1), nz) if way == 0 else lax.rem(z + (s - 1), nz)
        return pltpu.make_async_remote_copy(
            src_ref=wl.at[c] if first else wg.at[origin, c],
            dst_ref=wg.at[origin, c],
            send_sem=ag_send.at[way, s - 1, c],
            recv_sem=ag_recv.at[way, s - 1, c],
            device_id=(hop_to[way], b),
            device_id_type=MESH,
        )

    def wy_copy(d, rel):
        zo = lax.rem(z + rel, nz)
        return pltpu.make_async_remote_copy(
            src_ref=ws.at[d - 1, rel],
            dst_ref=wr.at[y, zo],
            send_sem=wy_send.at[d - 1, rel],
            recv_sem=wy_recv.at[d - 1, rel],
            device_id=(tile_at(d) * nz + z, b),
            device_id_type=MESH,
        )

    def gy_copy(d, rel):
        return pltpu.make_async_remote_copy(
            src_ref=gs.at[d - 1, rel],
            dst_ref=gr.at[d, rel],
            send_sem=gy_send.at[d - 1, rel],
            recv_sem=gy_recv.at[d - 1, rel],
            device_id=(tile_at(d) * nz + z, b),
            device_id_type=MESH,
        )

    def rs_copy(way, t, c):
        return pltpu.make_async_remote_copy(
            src_ref=rs.at[way, t, c],
            dst_ref=rr.at[way, t + 1, c],
            send_sem=rs_send.at[way, t, c],
            recv_sem=rs_recv.at[way, t, c],
            device_id=(hop_to[way], b),
            device_id_type=MESH,
        )

    def dx_copy(j):
        s = sender_of(j)
        return pltpu.make_async_remote_copy(
            src_ref=dxs.at[s],
            dst_ref=dx_hbm.at[0, pl.ds(pl.multiple_of(b * CG, CG), CG), :],
            send_sem=dx_send.at[j],
            recv_sem=dx_recv.at[j],
            device_id=(grid_id, s),
            device_id_type=MESH,
        )

    def dot_copy(j):
        return pltpu.make_async_remote_copy(
            src_ref=dots_s,
            dst_ref=dots_r.at[j],
            send_sem=dot_send.at[j],
            recv_sem=dot_recv.at[j],
            device_id=(grid_id, receiver_of(j)),
            device_id_type=MESH,
        )

    act_local(0).start()
    act_local(1).start()
    for j in range(1, nb):
        act_copy(0, jnp.int32(j)).start()
        act_copy(1, jnp.int32(j)).start()
    for way in (0, 1):
        for c in range(NSUB):
            if half > 1 or (c < NSUB // 2) == (way == 0):
                ag_copy(way, 1, c, True).start()

    lane = lax.broadcasted_iota(jnp.int32, (8, PIX), 1)
    column = lax.rem(lane, SIDE)
    row = lax.div(lane, SIDE)
    for t in range(TAPS):
        down, over = t // 3 - 1, t % 3 - 1
        inside = (row - down >= 0) & (row - down < SIDE) & (column - over >= 0) & (column - over < SIDE)
        tap_mask[t] = jnp.where(inside, 1.0, 0.0).astype(F32)
    tail_row = lax.div(lax.broadcasted_iota(jnp.int32, (CG, 128), 0), 16)
    tail_lane = lax.div(lax.broadcasted_iota(jnp.int32, (CG, 128), 1), CG)
    tail_mask[...] = jnp.where(lax.rem(tail_lane, 2) == tail_row, 1.0, 0.0).astype(F32)
    for k in range(2):
        tail_mask_bf[k] = jnp.where(tail_lane == 2 * k + tail_row, 1.0, 0.0).astype(F32).astype(BF)
    first_half = lax.broadcasted_iota(jnp.int32, (16, 128), 1) < 64
    parts[...] = jnp.zeros_like(parts)
    for c in range(NSUB):
        for way in (0, 1):
            rr[way, 0, c] = jnp.zeros((PR, 128), BF)
        rr[1 if c < NSUB // 2 else 0, 1, c] = jnp.zeros((PR, 128), BF)

    def expert_of(tile, zo):
        return lax.rem(tab_ref[tile, y * nz + zo], EXP)

    def pick(rel):
        zo = lax.rem(z + rel, nz)
        for e in range(EXP):
            at = e % 2 * MR
            block[e, :MR] = wg[zo, e // 2, at : at + MR, :]
            block[e, MR:] = wg[zo, e // 2, ES * MR :, :]
        wr[y, zo] = block[expert_of(y, zo)]
        for d in range(1, ny):
            ws[d - 1, rel] = block[expert_of(tile_at(d), zo)]

    def send_picks(rel):
        for d in range(1, ny):
            wy_copy(d, rel).start()

    def route_at(s, p, k):
        return (p * TOP + k) * nb + s

    def patch_lanes(p):
        return pl.ds(pl.multiple_of(p * PIX, PIX), PIX)

    def grad_patch(j, p):
        s = sender_of(j)
        index = s * pcol + p
        dy = dyg[s, :, patch_lanes(p)].astype(F32).reshape(CG // 8, 8, PIX)
        for t in range(TAPS):
            shift = ((t // 3 - 1) * SIDE + (t % 3 - 1)) % PIX
            moved = dy if shift == 0 else pltpu.roll(dy, shift, 2) * tap_mask[t][None]
            moved = moved.reshape(CG, PIX).astype(BF)
            if t < TAPS - 1:
                taps_buf[index, t * CG : (t + 1) * CG, :] = moved
            else:
                for k in range(4):
                    taps_buf[index, (t + k) * CG : (t + k + 1) * CG, :] = moved
        xp = xg[s, :, patch_lanes(p)]
        dims = (((1,), (1,)), ((), ()))
        main = lax.dot_general(xp, taps_buf[index, : 8 * CG, :], dims, preferred_element_type=F32)
        last = lax.dot_general(xp, taps_buf[index, 8 * CG :, :], dims, preferred_element_type=F32)
        last = last * tail_mask[...]
        gb[index, 0:32, :] = main[:, :128]
        gb[index, 32:64, :] = main[:, 128:]
        gb[index, 64:80, :] = last[:16] + last[16:]

    def grad_stage(rel):
        zo = lax.rem(z + rel, nz)
        for d in range(ny):
            route = lax.div(tab_ref[y, tile_at(d) * nz + zo], EXP)
            patch = lax.rem(route, nb) * pcol + lax.div(route, TOP * nb)
            value = (gb[patch] * gate_rows[pl.ds(route, 1), :]).astype(BF)
            if d == 0:
                gr[0, rel] = value
            else:
                gs[d - 1, rel] = value

    def route_unit(route):
        expert = rows_ref[y, route]
        owner = lax.div(expert, EXP)
        return wr[lax.div(owner, nz), lax.rem(owner, nz)], tail_mask_bf[lax.rem(expert, 2)]

    def dx_patch(j, p):
        s = sender_of(j)
        index = s * pcol + p
        mains, tails = [], []
        for k in range(TOP):
            unit, mask = route_unit(route_at(s, p, k))
            mains.append(jnp.concatenate([unit[0:32], unit[32:64]], axis=1))
            tails.append(jnp.concatenate([unit[64:80], unit[64:80]], axis=0) * mask)
        adjoint = jnp.dot(
            jnp.concatenate(mains, axis=0), taps_buf[index, : 8 * CG, :], preferred_element_type=F32
        ) + jnp.dot(
            jnp.concatenate(tails, axis=0), taps_buf[index, 8 * CG :, :], preferred_element_type=F32
        )
        xp = xg[s, :, patch_lanes(p)].astype(F32)
        total = jnp.zeros((CG, PIX), F32)
        for k in range(TOP):
            one = adjoint[k * CG : (k + 1) * CG]
            prod = xp * one
            prod = (prod[0:8] + prod[8:16]) + (prod[16:24] + prod[24:32])
            prod = prod[:, :128] + prod[:, 128:]
            parts[pl.ds(route_at(s, p, k), 1), :] = jnp.sum(prod, axis=0, keepdims=True)
            gate = gate_rows[pl.ds(route_at(s, p, k), 1), :]
            gate = jnp.concatenate([gate, gate], axis=1)
            total = total + (gate * one).astype(BF).astype(F32)
        dxs[s, :, patch_lanes(p)] = total.astype(BF)

    def own_piece(rel, c):
        zo = lax.rem(z + rel, nz)
        parts_of = [None] * 3
        for d in range(ny):
            expert = expert_of(lax.rem(y + ny - d, ny), zo)
            hits = [jnp.where(expert == c * ES + k, 1.0, 0.0).astype(F32) for k in range(ES)]
            main = gr[d, rel, :MR].astype(F32)
            last = gr[d, rel, MR:].astype(F32)
            terms = [main * hits[0], main * hits[1], last * jnp.where(first_half, hits[0], hits[1])]
            parts_of = [b if a is None else a + b for a, b in zip(parts_of, terms)]
        return parts_of

    piece_rows = (slice(0, MR), slice(MR, ES * MR), slice(ES * MR, PR))

    def rs_add(way, t, c, own):
        for rows, value in zip(piece_rows, own):
            rs[way, t, c, rows, :] = (value + rr[way, t, c, rows, :].astype(F32)).astype(BF)

    def wait_grads(rel):
        for d in range(1, ny):
            gy_copy(d, rel).wait_recv()

    wg[z] = wl[...]
    pick(jnp.int32(0))

    def gather_tick(k):
        s = lax.div(k, NSUB) + 1
        c = lax.rem(k, NSUB)
        low = c < NSUB // 2

        @pl.when(k < ticks)
        def _():
            for way in (0, 1):
                mine = low if way == 0 else jnp.logical_not(low)

                @pl.when(jnp.logical_or(s < half, mine))
                def _():
                    ag_copy(way, s, c, False).wait_recv()

                @pl.when(jnp.logical_or(s + 1 < half, jnp.logical_and(s + 1 == half, mine)))
                def _():
                    ag_copy(way, s + 1, c, False).start()

        turn = k - pick_from
        i = lax.div(turn, 2)

        @pl.when(jnp.logical_and(turn >= 0, jnp.logical_and(i * 2 == turn, i <= half)))
        def _():
            send_picks(i)

            @pl.when(jnp.logical_and(i > 0, i < half))
            def _():
                send_picks(nz - i)

        @pl.when(jnp.logical_and(k < ticks, c == NSUB - 1))
        def _():
            pick(s)

            @pl.when(s < half)
            def _():
                pick(nz - s)

    def grad_tick(j):
        @pl.when(j == 0)
        def _():
            act_local(0).wait()
            act_local(1).wait()

        @pl.when(j > 0)
        def _():
            act_copy(0, j).wait_recv()
            act_copy(1, j).wait_recv()

        def one(p, carry):
            grad_patch(j, p)
            return carry

        lax.fori_loop(0, pcol, one, 0)

    def stage_tick(k):
        count = nz // stage_ticks

        def rel_of(n):
            i = k * count + n
            return lax.rem(half + lax.div(i + 1, 2) * (1 - 2 * lax.rem(i, 2)) + nz, nz)

        def stage(n, carry):
            grad_stage(rel_of(n))
            return carry

        def send(n, carry):
            for d in range(1, ny):
                gy_copy(d, rel_of(n)).start()
            return carry

        lax.fori_loop(0, count, stage, 0)
        lax.fori_loop(0, count, send, 0)

    def scatter_start(k):
        t = lax.div(k, NSUB)
        c = lax.rem(k, NSUB)
        low = c < NSUB // 2

        @pl.when(c == 0)
        def _():
            wait_grads(half - t)

            @pl.when(t > 0)
            def _():
                wait_grads(nz - half + t)

        own = (own_piece(half - t, c), own_piece(nz - half + t, c))
        for way in (0, 1):
            mine = low if way == 0 else jnp.logical_not(low)

            @pl.when(jnp.logical_or(t > 1, jnp.logical_and(t == 1, mine)))
            def _():
                rs_copy(way, t - 1, c).wait_recv()

            rs_add(way, t, c, own[way])

    def scatter_send(k):
        t = lax.div(k, NSUB)
        c = lax.rem(k, NSUB)
        low = c < NSUB // 2
        for way in (0, 1):
            mine = low if way == 0 else jnp.logical_not(low)

            @pl.when(jnp.logical_or(t > 0, mine))
            def _():
                rs_copy(way, t, c).start()

    def wait_kernels(rel, carry):
        for d in range(1, ny):
            wy_copy(d, rel).wait_recv()
        return carry

    def phase_grad(k, carry):
        grad_tick(k)
        gather_tick(k)
        return carry

    def phase_stage(k, carry):
        gather_tick(k)

        @pl.when(k < stage_from + stage_ticks)
        def _():
            stage_tick(k - stage_from)

        return carry

    def phase_both(k, carry):
        gather_tick(k)
        scatter_start(k - rs_from)
        scatter_send(k - rs_from)
        return carry

    def phase_dx(k, carry):
        @pl.when(k < rs_end)
        def _():
            scatter_start(k - rs_from)

        j = nb - 1 - (k - dx_from)

        def one(p, carry):
            dx_patch(j, p)
            return carry

        @pl.when(j >= 0)
        def _():
            one(0, 0)

        @pl.when(k < rs_end)
        def _():
            scatter_send(k - rs_from)

        @pl.when(jnp.logical_and(j + 1 > 0, j + 1 < nb))
        def _():
            dx_copy(j + 1).start()

        @pl.when(j >= 0)
        def _():
            lax.fori_loop(1, pcol, one, 0)

        return carry

    lax.fori_loop(0, stage_from, phase_grad, 0)
    lax.fori_loop(stage_from, rs_from, phase_stage, 0)
    lax.fori_loop(rs_from, dx_from, phase_both, 0)
    lax.fori_loop(0, nz, wait_kernels, 0)
    lax.fori_loop(dx_from, all_ticks, phase_dx, 0)
    own_dx = pltpu.make_async_copy(
        dxs.at[b], dx_hbm.at[0, pl.ds(pl.multiple_of(b * CG, CG), CG), :], out_sem.at[0]
    )
    own_dx.start()
    dots = jnp.sum(parts[...].T, axis=0, keepdims=True).astype(BF).astype(F32)
    dots_s[...] = jnp.broadcast_to(dots, (8, 128))

    wait_grads(jnp.int32(0))
    last = half - 1
    for c in range(NSUB):
        for way in (0, 1):
            if half > 1 or (c < NSUB // 2) == (way == 0):
                rs_copy(way, last, c).wait_recv()
        if c == 0:
            for j in range(1, nb):
                dot_copy(jnp.int32(j)).start()
        value = [
            v + rr[0, half, c, rows, :].astype(F32) + rr[1, half, c, rows, :].astype(F32)
            for rows, v in zip(piece_rows, own_piece(jnp.int32(0), c))
        ]
        dw_v[ES * c, :MR] = value[0]
        dw_v[ES * c + 1, :MR] = value[1]
        dw_v[ES * c, MR:] = value[2]
        dw_v[ES * c + 1, MR:] = pltpu.roll(value[2], 64, 1)
    for h in range(2):
        for th in range(2):
            turns = [turned(dw_v[4 * h + el, th * CG : (th + 1) * CG, :]) for el in range(4)]
            for tl in range(4):
                value = turns[0][-tl % 4]
                for el in range(1, 4):
                    value = jnp.where(quarter == el, turns[el][(el - tl) % 4], value)
                flat_t[h, pl.ds(th * 4 + tl, CG, stride=TAPS), :] = value
        value = None
        for el in range(4):
            turns = turned(dw_v[4 * h + el, 64:80, :])
            both = jnp.concatenate([turns[el], turns[(el - 1) % 4]], axis=0)
            value = both if value is None else jnp.where(quarter == el, both, value)
        flat_t[h, pl.ds(8, CG, stride=TAPS), :] = value
    for h in range(2):
        for t in range(3):
            flat_a[t, h * 128 : (h + 1) * 128, :] = flat_t[h, t * 128 : (t + 1) * 128, :].T
    lane64 = lax.broadcasted_iota(jnp.int32, (8 * EXP, 128), 1)
    tiles = [None] * TAPS
    for ol in range(4):
        for t in range(3):
            piece = flat_a[t, pl.ds(ol, 8 * EXP, stride=4), :]
            if ol:
                piece = pltpu.roll(piece, CG * ol, 1)
            at = 2 * ol + t
            if t == 2:
                keep = (lane64 >= CG * ol) & (lane64 < CG * (ol + 1))
            else:
                keep = lane64 >= CG * ol
            tiles[at] = jnp.where(keep, piece, 0.0 if tiles[at] is None else tiles[at])
            if ol and t < 2:
                at += 1
                tiles[at] = jnp.where(lane64 < CG * ol, piece, 0.0 if tiles[at] is None else tiles[at])
    for q in range(TAPS):
        out_v[pl.ds(q, 8 * EXP, stride=TAPS), :] = tiles[q]
    out_dw = pltpu.make_async_copy(out_v, dw_hbm, out_sem.at[1])
    out_dw.start()

    total = dots_s[...]
    for j in range(1, nb):
        dot_copy(jnp.int32(j)).wait_recv()
        total = total + dots_r[j]
    total = gates * (1.0 - gates) * total[:1] * (1.0 / SIDE)
    for p in range(pcol):
        for k in range(TOP):
            spot = (p * TOP + k) * nb
            turn = total if spot == 0 else pltpu.roll(total, 128 - spot, 1)
            gg_ref[p, k : k + 1, :] = turn[:, :nb]

    for j in range(1, nb):
        act_copy(0, jnp.int32(j)).wait_send()
        act_copy(1, jnp.int32(j)).wait_send()
        dot_copy(jnp.int32(j)).wait_send()
        dx_copy(jnp.int32(j)).wait_send()
        dx_copy(jnp.int32(j)).wait_recv()

    def drain_ring(k, carry):
        s = lax.div(k, NSUB)
        c = lax.rem(k, NSUB)
        low = c < NSUB // 2
        for way in (0, 1):
            mine = low if way == 0 else jnp.logical_not(low)

            @pl.when(jnp.logical_or(s + 1 < half, mine))
            def _():
                ag_copy(way, s + 1, c, False).wait_send()

            @pl.when(jnp.logical_or(s > 0, mine))
            def _():
                rs_copy(way, s, c).wait_send()

        return carry

    lax.fori_loop(0, ticks, drain_ring, 0)

    def drain_rows(rel, carry):
        for d in range(1, ny):
            wy_copy(d, rel).wait_send()
            gy_copy(d, rel).wait_send()
        return carry

    lax.fori_loop(0, nz, drain_rows, 0)
    own_dx.wait()
    out_dw.wait()


def per_device(nz, inputs, cotangent, weights, gate_logits, routes):
    grid_size = lax.axis_size("grid")
    nb = lax.axis_size("batch")
    ny = grid_size // nz
    half = nz // 2
    _, channels, width = inputs.shape
    pcol = width // PIX
    patches = nb * pcol
    count = patches * TOP
    index = lax.axis_index("grid")
    y, z = index // nz, index % nz

    near = routes.reshape(nb, ny, nz, pcol, TOP)
    near = lax.dynamic_index_in_dim(near, z, 2, keepdims=False)
    rows = near.transpose(1, 2, 3, 0).reshape(ny, count)
    code = jnp.arange(count, dtype=jnp.int32)[None, :] * EXP + rows % EXP
    named = (rows // EXP)[:, None, :] == jnp.arange(grid_size, dtype=jnp.int32)[None, :, None]
    table = jnp.sum(jnp.where(named, code[:, None, :], 0), axis=2)
    own = lax.dynamic_slice_in_dim(gate_logits, index * pcol, pcol, 1).transpose(1, 2, 0).reshape(1, count)
    logits = jnp.pad(own, ((0, 0), (0, 128 - count)))

    vmem, smem, hbm = (
        pl.BlockSpec(memory_space=pltpu.VMEM),
        pl.BlockSpec(memory_space=pltpu.SMEM),
        pl.BlockSpec(memory_space=pl.ANY),
    )
    dma = pltpu.SemaphoreType.DMA
    d_inputs, d_flat, grads = pl.pallas_call(
        functools.partial(step_kernel, ny, nz, nb, pcol),
        out_shape=(
            jax.ShapeDtypeStruct(inputs.shape, BF),
            jax.ShapeDtypeStruct((EXP * ROW // 4, 128), F32),
            jax.ShapeDtypeStruct((pcol, TOP, nb), F32),
        ),
        in_specs=[hbm, hbm, vmem, smem, smem, vmem],
        out_specs=(hbm, hbm, vmem),
        scratch_shapes=[
            pltpu.VMEM((nb, CG, width), BF),
            pltpu.VMEM((nb, CG, width), BF),
            pltpu.VMEM((patches, 12 * CG, PIX), BF),
            pltpu.VMEM((nz, NSUB, PR, 128), BF),
            pltpu.VMEM((ny - 1, nz, UR, 128), BF),
            pltpu.VMEM((ny, nz, UR, 128), BF),
            pltpu.VMEM((patches, UR, 128), F32),
            pltpu.VMEM((ny - 1, nz, UR, 128), BF),
            pltpu.VMEM((ny, nz, UR, 128), BF),
            pltpu.VMEM((2, half + 1, NSUB, PR, 128), BF),
            pltpu.VMEM((2, half, NSUB, PR, 128), BF),
            pltpu.VMEM((nb, CG, width), BF),
            pltpu.VMEM((128, 128), F32),
            pltpu.VMEM((8, 128), F32),
            pltpu.VMEM((nb, 8, 128), F32),
            pltpu.VMEM((EXP, UR, 128), F32),
            pltpu.VMEM((TAPS, 8, PIX), F32),
            pltpu.VMEM((CG, 128), F32),
            pltpu.VMEM((2, CG, 128), BF),
            pltpu.VMEM((EXP, UR, 128), BF),
            pltpu.VMEM((NSUB, PR, 128), BF),
            pltpu.VMEM((3, EXP * CG, 128), F32),
            pltpu.VMEM((2, 3 * 128, 128), F32),
            pltpu.VMEM((EXP * ROW // 4, 128), F32),
            pltpu.VMEM((128, 128), F32),
            dma((2, nb)), dma((2, nb)), dma((2,)),
            dma((2, half, NSUB)), dma((2, half, NSUB)),
            dma((ny - 1, nz)), dma((ny - 1, nz)),
            dma((ny - 1, nz)), dma((ny - 1, nz)),
            dma((2, half, NSUB)), dma((2, half, NSUB)),
            dma((nb,)), dma((nb,)), dma((nb,)), dma((nb,)), dma((2,)),
        ],
        compiler_params=pltpu.CompilerParams(collective_id=0, has_side_effects=True),
        name="expert_step",
    )(inputs, cotangent, weights.reshape(EXP, CG * ROW), table, rows, logits)

    d_weights = (d_flat * (1.0 / SIDE)).reshape(weights.shape)
    gate_grad = grads.transpose(2, 0, 1)
    return (d_inputs, d_weights, gate_grad)


def solution(mesh):
    grid_size = mesh.shape["grid"]
    nz = Z_SIZE if grid_size % Z_SIZE == 0 else grid_size // 2
    placed = (
        P("batch", None, "grid"),
        P("batch", None, "grid"),
        P("grid", "batch", None),
        P(),
        P(),
    )
    return jax.shard_map(
        functools.partial(per_device, nz),
        mesh=mesh,
        in_specs=placed,
        out_specs=(P("batch", None, "grid"), P("grid", "batch", None), P(None, "grid", None)),
        check_vma=False,
    )
```
